32 devices in a mesh: shard: 16 (over z, y, x), head: 2 (over core).
Axes of the slice: x: 2, y: 2, z: 4, core: 2. Of those that a mesh axis runs over, the one named last changes fastest.
Arguments:
- queries: bfloat16 [8192, 2048], P('shard', 'head'), may hold values from -170 to 170
- key_weight: bfloat16 [1024, 2048], P('shard', 'head'), may hold values from -0.1875 to 0.1875
- value_weight: bfloat16 [1024, 2048], P('shard', 'head'), may hold values from -0.1875 to 0.1875
- out_weight: bfloat16 [4096, 2048], P(None, 'head'), may hold values from -0.5 to 0.5
- database: bfloat16 [64, 128, 1024], P('shard', 'head'), may hold values from -6 to 6
- neighbours: int32 [128, 2], replicated, may hold values from 0 to 63, as said below
- placement: int32 [64], replicated, may hold values from 0 to 63, as said below
Outputs:
- mixed: bfloat16 [8192, 4096], P('shard', 'head')
The draws below stay inside these ranges and needn't reach their ends.
Inputs may be any that keep to these rules, and one draw needn't show every extreme that they name: `placement`: each storage slot appears once; slot s is stored on index s // 4 of shard. The 16 neighbours of the groups of one index of shard have storage slots on pairwise different indices of shard.
All inputs are finite; a program needn't handle non-finite values.
Results may differ from the reference program's by a relative error of at most 0.012.
The reference program's roundings to bfloat16 on the way count: a program that leaves them out, or rounds other values in their place, can miss the bound.
Values may be sent and summed in bfloat16 or wider, within the bound.
A program may use at most 128 MiB of HBM per device.

```python
import jax
import jax.numpy as jnp
from jax import lax

D = 4096
HEADS = 16
HD = 128
DE = 1024
CH = 64
KNB = 2
R = 128
CH_DEV = 8
BLK_PER = 4
SEQ = 512
TOKENS = 8192
GROUPS = 128
NBLOCKS = 64
HDIM = 2048
N_SHARD = 16


def draw_queries(key, part):
    shape = (TOKENS, HEADS * HD)
    return jax.random.truncated_normal(key, -4.0, 4.0, shape, jnp.float32).astype(jnp.bfloat16)


def retrieval_tables(key):
    perm = jax.random.permutation(jax.random.fold_in(key, 11), NBLOCKS).astype(jnp.int32)
    source_weight = jax.random.randint(jax.random.fold_in(key, 12), (N_SHARD,), 1, 5).astype(jnp.int32)
    raw_score = jax.random.randint(jax.random.fold_in(key, 13), (N_SHARD, N_SHARD), 0, 1 << 20).astype(jnp.int32)
    score = raw_score * source_weight[None, :] * 128 + jnp.arange(N_SHARD, dtype=jnp.int32)[None, :]
    picks = KNB * CH_DEV
    unused, sources = lax.top_k(score, picks)
    sources = sources.astype(jnp.int32)
    within = jax.random.randint(jax.random.fold_in(key, 14), (N_SHARD, picks), 0, BLK_PER).astype(jnp.int32)
    slots = (sources * BLK_PER + within).reshape(GROUPS, KNB)
    inverse = jnp.zeros((NBLOCKS,), jnp.int32).at[perm].set(jnp.arange(NBLOCKS, dtype=jnp.int32))
    ids = inverse[slots].astype(jnp.int32)
    return (ids, perm)


def draw_neighbours(key, part):
    return retrieval_tables(key)[0]


def draw_placement(key, part):
    return retrieval_tables(key)[1]


def shard_levels(key, dims, shards, smallest, largest):
    def one(axis_at, blocks):
        steps = jax.random.uniform(jax.random.fold_in(jax.random.fold_in(key, 6), axis_at), (blocks,), jnp.float32, smallest / len(shards), largest / len(shards))
        return jnp.repeat(jnp.exp(steps), dims[axis_at] // blocks).reshape((-1,) + (1,) * (len(dims) - axis_at - 1))

    level = one(*shards[0])
    for cut in shards[1:]:
        level = level * one(*cut)
    return level


def gaussian(own_key, dims, spread, limit, shards=(), kind=jnp.bfloat16):
    array = spread * jax.random.normal(own_key, dims, jnp.float32)
    if shards:
        array = array * shard_levels(own_key, dims, shards, -0.22, 0.18)
    return jnp.clip(array, -limit, limit).astype(kind)


def setup_inputs(seed: int = 0) -> dict:
    seeds = jax.random.split(jax.random.key(seed), 8)
    queries = draw_queries(jax.random.fold_in(seeds[7], 71), 0)
    key_weight = gaussian(seeds[1], (DE, HDIM), DE ** -0.5, 0.1875, ((0, 16), (1, 2)))
    value_weight = gaussian(seeds[2], (DE, HDIM), DE ** -0.5, 0.1875, ((0, 16), (1, 2)))
    out_weight = gaussian(seeds[3], (D, HDIM), HD ** -0.5, 0.5, ((1, 2),))
    database = gaussian(seeds[4], (NBLOCKS, R, DE), 1.0, 6.0, ((0, 16), (1, 2)))
    neighbours = draw_neighbours(jax.random.fold_in(seeds[7], 71), 0)
    placement = draw_placement(jax.random.fold_in(seeds[7], 71), 0)
    return {"queries": queries, "key_weight": key_weight, "value_weight": value_weight, "out_weight": out_weight, "database": database, "neighbours": neighbours, "placement": placement}


def reference(queries, key_weight, value_weight, out_weight, database, neighbours, placement):
    head_width = HEADS * HD
    seq_count = TOKENS // SEQ
    score_scale = HD ** -0.5
    block_rows = placement[neighbours].astype(jnp.int32)
    query_seq = queries.reshape(seq_count, SEQ, head_width)
    query_pad = jnp.concatenate([query_seq[:, CH - 1:], jnp.zeros((seq_count, CH - 1, head_width), jnp.bfloat16)], axis=1)
    query_pad = query_pad.reshape(GROUPS, CH, HEADS, HD)

    def one_group(pair_args):
        query_win, slot_pair = pair_args
        encoded = database[slot_pair].reshape(KNB * R, DE)
        key_rows = jnp.dot(encoded, key_weight, preferred_element_type=jnp.float32).astype(jnp.bfloat16)
        val_rows = jnp.dot(encoded, value_weight, preferred_element_type=jnp.float32).astype(jnp.bfloat16)
        key_rows = key_rows.reshape(KNB * R, HEADS, HD)
        val_rows = val_rows.reshape(KNB * R, HEADS, HD)
        scores = jnp.einsum("whd,khd->hwk", query_win.astype(jnp.float32), key_rows.astype(jnp.float32)) * score_scale
        row_max = jnp.max(scores, axis=-1, keepdims=True)
        expo = jnp.exp(scores - row_max)
        probs = expo / jnp.sum(expo, axis=-1, keepdims=True)
        weights_bf = probs.astype(jnp.bfloat16)
        window_out = jnp.einsum("hwk,khd->whd", weights_bf.astype(jnp.float32), val_rows.astype(jnp.float32))
        return window_out.astype(jnp.bfloat16).reshape(CH, head_width)

    windows = lax.map(one_group, (query_pad, block_rows))
    windows = windows.reshape(seq_count, SEQ, head_width)
    attention = jnp.concatenate([jnp.zeros((seq_count, CH - 1, head_width), jnp.bfloat16), windows[:, :SEQ - (CH - 1)]], axis=1)
    attention = attention.reshape(TOKENS, head_width)
    mixed_out = lax.dot_general(attention, out_weight, (((1,), (1,)), ((), ())), preferred_element_type=jnp.float32)
    return mixed_out.astype(jnp.bfloat16)
```

```python
import jax
import jax.numpy as jnp
from jax import lax
from jax.experimental import pallas as pl
from jax.experimental.pallas import tpu as pltpu
from jax.sharding import PartitionSpec as P

HD = 128
CH = 64
KNB = 2
NZ, NY, NX = 4, 2, 2
PLANE = NY * NX
EDGE = 16
WINDOW = CH + EDGE
Z_PARTS = 4
E_PARTS = 2
OUT_TILE = 256
MESH = pl.DeviceIdType.MESH
VMEM_LIMIT = 60 * 1024 * 1024
NT = (((1,), (1,)), ((), ()))


def shifted(shard, dy, dx):
    z, y, x = shard // PLANE, (shard // NX) % NY, shard % NX
    return z * PLANE + ((y + dy) % NY) * NX + (x + dx) % NX


def fused_kernel(
    near_ref, place_ref, q_ref, kw_ref, vw_ref, ow_ref, db_ref,
    out_ref,
    w, sets, e_out, e_in, kk, vv, q_pad, part_o, part_m, part_l, att, ow_own, ow_other, out_v,
    s_send, s_recv, a_send, a_recv, f_send, f_recv, z_send, p_send, g_send, w_recv, o_sem,
    t_send, t_recv, l_sem, out_sem, z_ready,
):
    s = lax.axis_index("shard")
    h = lax.axis_index("head")
    z, y, x = s // PLANE, (s // NX) % NY, s % NX
    near_x = s + 1 - 2 * x
    near_y = s + NX * (1 - 2 * y)
    n = NZ * PLANE
    groups, _, width = q_ref.shape
    blk, half, de = db_ref.shape
    feats = ow_own.shape[0]
    picks = near_ref.shape[0] * near_ref.shape[1] // n
    is_end = (z == 0) | (z == NZ - 1)

    barrier = pltpu.get_barrier_semaphore()

    def greet(to, head):
        pl.semaphore_signal(barrier, inc=1, device_id=(to, head), device_id_type=MESH)

    for j in range(1, PLANE):
        greet(shifted(s, j // NX, j % NX), h)
    greet(s, 1 - h)

    @pl.when((z == 0) | (z == 1))
    def _():
        greet(s + PLANE, h)

    @pl.when((z == 2) | (z == 3))
    def _():
        greet(s - PLANE, h)

    loads = [
        pltpu.make_async_copy(kw_ref, w.at[0, s], l_sem.at[0]),
        pltpu.make_async_copy(vw_ref, w.at[1, s], l_sem.at[1]),
        pltpu.make_async_copy(db_ref, sets.at[z], l_sem.at[2]),
        pltpu.make_async_copy(q_ref, q_pad.at[pl.ds(0, groups)], l_sem.at[3]),
        pltpu.make_async_copy(ow_ref.at[pl.ds(h * feats, feats)], ow_own, l_sem.at[4]),
    ]
    for load in loads:
        load.start()
    q_pad[groups] = jnp.zeros((CH, width), jnp.bfloat16)
    for load in loads[:3]:
        load.wait()

    @pl.when(is_end)
    def _():
        pl.semaphore_wait(barrier, PLANE)

    @pl.when(~is_end)
    def _():
        pl.semaphore_wait(barrier, PLANE + 2)

    @pl.when(z == 1)
    def _():
        pl.semaphore_signal(z_ready, inc=1, device_id=(s - PLANE, h), device_id_type=MESH)

    @pl.when(z == 2)
    def _():
        pl.semaphore_signal(z_ready, inc=1, device_id=(s + PLANE, h), device_id_type=MESH)

    def weight_copy(kind, chunk, to, sem):
        return pltpu.make_async_remote_copy(
            src_ref=w.at[kind, chunk], dst_ref=w.at[kind, chunk], send_sem=sem,
            recv_sem=w_recv.at[kind, chunk], device_id=(to, h), device_id_type=MESH)

    def column(zz):
        return zz * PLANE + y * NX + x

    def up_copy(kind, zz):
        return weight_copy(kind, column(zz), s + PLANE, z_send.at[0, kind, zz])

    def down_copy(kind, zz):
        return weight_copy(kind, column(zz), s - PLANE, z_send.at[1, kind, zz])

    def x_copy(kind, zz):
        return weight_copy(kind, column(zz), near_x, p_send.at[0, kind, zz])

    def y_copy(kind, zz):
        return weight_copy(kind, column(zz), near_y, p_send.at[1, kind, zz])

    def diag_k(zz):
        return weight_copy(0, zz * PLANE + y * NX + 1 - x, near_y, g_send.at[0, zz])

    def diag_v(zz):
        return weight_copy(1, zz * PLANE + (1 - y) * NX + x, near_x, g_send.at[1, zz])

    def arrive(kind, chunk):
        weight_copy(kind, chunk, near_x, z_send.at[0, 0, 0]).wait_recv()

    z_rows = half // Z_PARTS
    e_rows = half // E_PARTS

    def set_copy(way, zz, r):
        part = sets.at[zz, :, pl.ds(r * z_rows, z_rows)]
        return pltpu.make_async_remote_copy(
            src_ref=part, dst_ref=part, send_sem=s_send.at[way, zz, r], recv_sem=s_recv.at[zz, r],
            device_id=(s + PLANE - 2 * PLANE * way, h), device_id_type=MESH)

    def enc_copy(zz, j, r):
        d = zz * PLANE + j
        rows = pl.ds(r * e_rows, e_rows)
        return pltpu.make_async_remote_copy(
            src_ref=e_out.at[d, rows], dst_ref=e_in.at[d, h, rows], send_sem=a_send.at[d, r],
            recv_sem=a_recv.at[d, r], device_id=(shifted(s, j // NX, j % NX), h),
            device_id_type=MESH)

    def half_copy(d, r, head):
        piece = e_in.at[d, head, pl.ds(r * e_rows, e_rows)]
        return pltpu.make_async_remote_copy(
            src_ref=piece, dst_ref=piece, send_sem=f_send.at[d, r], recv_sem=f_recv.at[d, r],
            device_id=(s, 1 - h), device_id_type=MESH)

    def out_copy():
        return pltpu.make_async_remote_copy(
            src_ref=ow_ref.at[pl.ds((1 - h) * feats, feats)], dst_ref=ow_other,
            send_sem=o_sem.at[0], recv_sem=o_sem.at[1], device_id=(s, 1 - h),
            device_id_type=MESH)

    def swap(c):
        rows = pl.ds(c * CH, CH)
        return pltpu.make_async_remote_copy(
            src_ref=att.at[0, rows], dst_ref=att.at[1, rows], send_sem=t_send.at[c],
            recv_sem=t_recv.at[c], device_id=(s, 1 - h), device_id_type=MESH)

    def pick(to, i):
        return place_ref[near_ref[i % KNB, to * (picks // KNB) + i // KNB]]

    def find(j):
        to = shifted(s, j // NX, j % NX)
        found = [jnp.int32(0)] * NZ
        for i in range(picks):
            slot = pick(to, i)
            owner, block = slot // blk, slot % blk
            found = [
                got + jnp.where(owner == column(zz), block, 0) for zz, got in enumerate(found)]
        return found

    def slot_of(i):
        own = pick(s, i) // blk
        return own // PLANE * PLANE + (y + own // NX) % NY * NX + (x + own) % NX

    def both(k, act):
        if k == 0:
            act(z)
            return

        @pl.when(z >= k)
        def _():
            act(z - k)

        @pl.when(z + k < NZ)
        def _():
            act(z + k)

    def onward(zz, up, down):
        @pl.when((zz <= z) & (z < NZ - 1))
        def _():
            up()

        @pl.when((zz >= z) & (z > 0))
        def _():
            down()

    def send_on(kind, zz):
        onward(zz, lambda: up_copy(kind, zz).start(), lambda: down_copy(kind, zz).start())

    def send_set(zz, parts):
        for r in parts:
            onward(zz, lambda: set_copy(0, zz, r).start(), lambda: set_copy(1, zz, r).start())

    def weights_in(kind, k):
        def act(zz):
            arrive(kind, column(zz))
            send_on(kind, zz)
            x_copy(kind, zz).start()
            y_copy(kind, zz).start()
        both(k, act)

    def turn_k(k):
        def act(zz):
            arrive(0, zz * PLANE + y * NX + 1 - x)
            diag_k(zz).start()
        both(k, act)

    def turn_v(k):
        def act(zz):
            arrive(1, zz * PLANE + (1 - y) * NX + x)
            diag_v(zz).start()
        both(k, act)

    def set_in(k, parts):
        def act(zz):
            for r in parts:
                set_copy(0, zz, r).wait_recv()
                send_set(zz, [r])
        both(k, act)

    def spread(zz, r):
        rows = pl.ds(r * e_rows, e_rows)

        def taken(j):
            block = chosen(zz, j)
            got = sets[zz, 0, rows]
            for b in range(1, blk):
                got = lax.select(block == b, sets[zz, b, rows], got)
            return got

        for j in range(1, PLANE):
            e_out[zz * PLANE + j, rows] = taken(j)
            enc_copy(zz, j, r).start()
        e_in[zz * PLANE, h, rows] = taken(0)
        half_copy(zz * PLANE, r, h).start()

    def spread_in(k, r):
        def act(zz):
            for part in range(r * Z_PARTS // E_PARTS, (r + 1) * Z_PARTS // E_PARTS):
                set_copy(0, zz, part).wait_recv()
            spread(zz, r)
        both(k, act)

    for kind in range(2):
        x_copy(kind, z).start()
        y_copy(kind, z).start()

    @pl.when(~is_end)
    def _():
        for kind in range(2):
            send_on(kind, z)
        send_set(z, [0])

    out_copy().start()
    blocks = [find(j) for j in range(PLANE)]
    slots = [slot_of(i) for i in range(picks)]

    def chosen(zz, j):
        return sum(jnp.where(zz == i, got, 0) for i, got in enumerate(blocks[j]))

    @pl.when(is_end)
    def _():
        turn_k(0)
        turn_v(0)
        for r in range(E_PARTS):
            spread(z, r)
        pl.semaphore_wait(z_ready, 1)
        for kind in range(2):
            send_on(kind, z)
        send_set(z, range(Z_PARTS))
        weights_in(0, 1)
        weights_in(1, 1)
        turn_k(1)
        weights_in(0, 2)
        turn_v(1)
        weights_in(1, 2)
        turn_k(2)
        weights_in(0, 3)
        turn_v(2)
        weights_in(1, 3)
        spread_in(1, 0)
        turn_k(3)
        spread_in(1, 1)
        turn_v(3)

    @pl.when(~is_end)
    def _():
        weights_in(0, 1)
        turn_k(0)
        weights_in(1, 1)
        send_set(z, [1])
        turn_v(0)
        weights_in(0, 2)
        turn_k(1)
        weights_in(1, 2)
        send_set(z, [2, 3])
        turn_v(1)
        set_in(1, range(Z_PARTS))
        turn_k(2)
        set_in(2, range(0, Z_PARTS // 2))
        turn_v(2)
        set_in(2, range(Z_PARTS // 2, Z_PARTS))
        for k in range(NZ - 1):
            for r in range(E_PARTS):
                both(k, lambda zz: spread(zz, r))

    def weights_complete():
        for zz in range(NZ):
            arrive(1, zz * PLANE + y * NX + 1 - x)
            arrive(0, zz * PLANE + (1 - y) * NX + x)
            for kind in range(2):
                arrive(kind, zz * PLANE + (1 - y) * NX + 1 - x)

    def weights_sent():
        for zz in range(NZ):
            for kind in range(2):
                onward(zz, lambda: up_copy(kind, zz).wait_send(), lambda: down_copy(kind, zz).wait_send())
                x_copy(kind, zz).wait_send()
                y_copy(kind, zz).wait_send()
            diag_k(zz).wait_send()
            diag_v(zz).wait_send()

    def plane_at(p):
        order = (
            range(NZ), (1, 0, 2, 3), (2, 3, 1, 0), range(NZ - 1, -1, -1))
        zz = jnp.int32(0)
        for place, planes in enumerate(order):
            zz = jnp.where(z == place, planes[p], zz)
        return zz

    def pass_halves(zz, r):
        for j in range(1, PLANE):
            enc_copy(zz, j, r).wait_recv()
            half_copy(zz * PLANE + j, r, h).start()

    def halves_in(zz, r):
        for j in range(PLANE):
            half_copy(zz * PLANE + j, r, 1 - h).wait_recv()

    tile = 256

    def project(zz, first, count):
        slab = pl.ds(zz * PLANE, PLANE)
        rows = pl.ds(first, count)

        @pl.loop(0, width // tile)
        def _(c):
            cols = pl.ds(pl.multiple_of(c * tile, tile), tile)
            enc = e_in[slab, :, rows].reshape(PLANE * 2 * count, de)
            for kind, dst in ((0, kk), (1, vv)):
                weight = w[kind, :, :, cols].reshape(de, tile)
                got = jnp.dot(enc, weight, preferred_element_type=jnp.float32)
                dst[:, :, rows, cols] = got.astype(jnp.bfloat16).reshape(PLANE, 2, count, tile)

    scale = HD ** -0.5
    heads = width // HD

    def attend(zz):
        @pl.loop(0, PLANE)
        def _(j):
            d = zz * PLANE + j
            group = jnp.int32(0)
            for i, slot in enumerate(slots):
                group = jnp.where(slot == d, i // KNB, group)
            batch = 4
            for first in range(0, heads, batch):
                spans = [slice(i * HD, (i + 1) * HD) for i in range(first, first + batch)]
                scores = [
                    lax.dot_general(
                        jnp.concatenate(
                            [q_pad[group, CH - EDGE:, cols], q_pad[group + 1, :, cols]], axis=0),
                        kk[j, :, :, cols].reshape(2 * half, HD), NT,
                        preferred_element_type=jnp.float32) * scale
                    for cols in spans]
                tops = [jnp.max(score, axis=1, keepdims=True) for score in scores]
                expos = [jnp.exp(score - top) for score, top in zip(scores, tops)]
                sums = [jnp.sum(expo, axis=1, keepdims=True) for expo in expos]
                outs = [
                    jnp.dot(expo.astype(jnp.bfloat16), vv[j, :, :, cols].reshape(2 * half, HD),
                            preferred_element_type=jnp.float32)
                    for expo, cols in zip(expos, spans)]
                for cols, top, total, got in zip(spans, tops, sums, outs):
                    part_o[d, :, cols] = got
                    part_m[d, :, cols] = jnp.broadcast_to(top, (WINDOW, HD))
                    part_l[d, :, cols] = jnp.broadcast_to(total, (WINDOW, HD))

    def combine(c):
        one, two = slot_of(KNB * c), slot_of(KNB * c + 1)
        last = lax.broadcasted_iota(jnp.int32, (EDGE, HD), 0) == EDGE - 1
        for head in range(heads):
            cols = slice(head * HD, (head + 1) * HD)
            top = jnp.maximum(part_m[one, :, cols], part_m[two, :, cols])
            left = jnp.exp(part_m[one, :, cols] - top)
            right = jnp.exp(part_m[two, :, cols] - top)
            total = part_l[one, :, cols] * left + part_l[two, :, cols] * right
            got = (part_o[one, :, cols] * left + part_o[two, :, cols] * right) / total
            edge = pl.ds(pl.multiple_of(c * CH + CH - EDGE, EDGE), EDGE)
            old = att[0, edge, cols].astype(jnp.float32)
            att[0, edge, cols] = jnp.where(last, got[:EDGE], old).astype(jnp.bfloat16)

            @pl.when(c < groups - 1)
            def _():
                att[0, pl.ds(pl.multiple_of(c * CH + CH, CH), CH), cols] = got[EDGE:].astype(jnp.bfloat16)

    att[0, 0:CH] = jnp.zeros((CH, width), jnp.bfloat16)
    loads[3].wait()
    for p in range(NZ):
        zz = plane_at(p)
        if p == 0:
            for r in range(E_PARTS):
                pass_halves(zz, r)
            weights_complete()
        elif p < NZ - 1:
            for r in range(E_PARTS):
                pass_halves(zz, r)
        if p < NZ - 1:
            for r in range(E_PARTS):
                halves_in(zz, r)
            project(zz, 0, half)
        else:
            for r in range(E_PARTS):
                pass_halves(zz, r)
                halves_in(zz, r)
                project(zz, r * e_rows, e_rows)

        @pl.when(is_end)
        def _():
            if p == 1:
                spread_in(2, 1)
            if p == 2:
                spread_in(3, 0)
        attend(zz)

        @pl.when(is_end)
        def _():
            if p == 0:
                spread_in(2, 0)
            if p == 2:
                spread_in(3, 1)
        if p == 0:
            weights_sent()

    @pl.loop(0, groups)
    def _(c):
        combine(c)
        swap(c).start()

    def out_tile(t):
        return pltpu.make_async_copy(
            out_v.at[:, pl.ds(t * OUT_TILE, OUT_TILE)], out_ref.at[:, pl.ds(t * OUT_TILE, OUT_TILE)],
            out_sem.at[t])

    def mix(t, side, held):
        rows = pl.ds(pl.multiple_of(t * OUT_TILE, OUT_TILE), OUT_TILE)
        return lax.dot_general(att[side], held[rows], NT, preferred_element_type=jnp.float32)

    loads[4].wait()
    mine = mix(0, 0, ow_own)
    out_copy().wait()
    for c in range(groups):
        swap(c).wait_recv()
    out_v[:, 0:OUT_TILE] = (mine + mix(0, 1, ow_other)).astype(jnp.bfloat16)
    out_tile(0).start()

    @pl.loop(1, feats // OUT_TILE)
    def _(t):
        got = mix(t, 0, ow_own) + mix(t, 1, ow_other)
        out_v[:, pl.ds(pl.multiple_of(t * OUT_TILE, OUT_TILE), OUT_TILE)] = got.astype(jnp.bfloat16)
        out_tile(t).start()

    for zz in range(NZ):
        for r in range(Z_PARTS):
            onward(zz, lambda: set_copy(0, zz, r).wait_send(), lambda: set_copy(1, zz, r).wait_send())
        for j in range(PLANE):
            for r in range(E_PARTS):
                if j:
                    enc_copy(zz, j, r).wait_send()
                half_copy(zz * PLANE + j, r, h).wait_send()
    for c in range(groups):
        swap(c).wait_send()
    for t in range(feats // OUT_TILE):
        out_tile(t).wait()


def local_small(queries, key_weight, value_weight, out_weight, database, neighbours, placement):
    n = NZ * PLANE
    tok, width = queries.shape
    blk, half, de = database.shape
    feats = out_weight.shape[0] // 2
    groups = tok // CH
    sm = pl.BlockSpec(memory_space=pltpu.SMEM)
    hbm = pl.BlockSpec(memory_space=pl.ANY)
    dma = pltpu.SemaphoreType.DMA
    bf16 = jnp.bfloat16
    return pl.pallas_call(
        fused_kernel,
        out_shape=jax.ShapeDtypeStruct((tok, feats), bf16),
        in_specs=[sm, sm] + [hbm] * 5,
        out_specs=hbm,
        scratch_shapes=[
            pltpu.VMEM((2, n) + key_weight.shape, bf16),
            pltpu.VMEM((NZ,) + database.shape, bf16),
            pltpu.VMEM((n, half, de), bf16),
            pltpu.VMEM((n, 2, half, de), bf16),
            pltpu.VMEM((PLANE, 2, half, width), bf16),
            pltpu.VMEM((PLANE, 2, half, width), bf16),
            pltpu.VMEM((groups + 1, CH, width), bf16),
            *[pltpu.VMEM((n, WINDOW, width), jnp.float32)] * 3,
            pltpu.VMEM((2, tok, width), bf16),
            pltpu.VMEM((feats, width), bf16),
            pltpu.VMEM((feats, width), bf16),
            pltpu.VMEM((tok, feats), bf16),
            dma((2, NZ, Z_PARTS)), dma((NZ, Z_PARTS)), dma((n, E_PARTS)), dma((n, E_PARTS)),
            dma((n, E_PARTS)), dma((n, E_PARTS)), dma((2, 2, NZ)), dma((2, 2, NZ)), dma((2, NZ)),
            dma((2, n)), dma((2,)), dma((groups,)), dma((groups,)), dma((5,)),
            dma((feats // OUT_TILE,)), pltpu.SemaphoreType.REGULAR,
        ],
        compiler_params=pltpu.CompilerParams(
            collective_id=0, has_side_effects=True, vmem_limit_bytes=VMEM_LIMIT),
    )(neighbours.T, placement, queries.reshape(groups, CH, width), key_weight, value_weight, out_weight, database)


def local_general(queries, key_weight, value_weight, out_weight, database, neighbours, placement):
    shard_count = lax.axis_size("shard")
    shard_self = lax.axis_index("shard")
    tok_rows = queries.shape[0]
    hd_local = queries.shape[1]
    heads_local = hd_local // HD
    per_dev = tok_rows // CH
    blk_local = database.shape[0]
    slots = placement[neighbours]
    needed = slots.reshape(shard_count, per_dev * KNB)
    owners = needed // blk_local
    matches = owners == shard_self
    hits = jnp.any(matches, axis=1)
    which = jnp.sum(jnp.where(matches, needed % blk_local, 0), axis=1)
    outgoing = jnp.zeros((shard_count,) + database.shape[1:], jnp.bfloat16)
    for b in range(blk_local):
        taken = (hits & (which == b))[:, None, None]
        outgoing = jnp.where(taken, database[b][None], outgoing)
    arrived = lax.all_to_all(outgoing, "shard", split_axis=0, concat_axis=0, tiled=True)
    own_need = lax.dynamic_slice_in_dim(needed, shard_self, 1, 0)[0]
    half_rows = jnp.concatenate(
        [
            lax.dynamic_slice_in_dim(arrived, own_need[i] // blk_local, 1, 0)
            for i in range(per_dev * KNB)
        ],
        axis=0,
    )
    encoded = lax.all_gather(half_rows, "head", axis=1, tiled=True)
    key_rows, val_rows = (
        lax.all_gather(key_weight, "shard", axis=0, tiled=True),
        lax.all_gather(value_weight, "shard", axis=0, tiled=True),
    )
    key_block = jnp.einsum(
        "brd,de->bre", encoded, key_rows, preferred_element_type=jnp.float32
    ).astype(jnp.bfloat16)
    val_block = jnp.einsum(
        "brd,de->bre", encoded, val_rows, preferred_element_type=jnp.float32
    ).astype(jnp.bfloat16)
    neighbour_len = encoded.shape[1]
    key_heads = key_block.reshape(per_dev, KNB * neighbour_len, heads_local, HD)
    val_heads = val_block.reshape(per_dev, KNB * neighbour_len, heads_local, HD)
    query_pad = jnp.concatenate(
        [queries[CH - 1 :], jnp.zeros((CH - 1, hd_local), jnp.bfloat16)], axis=0
    )
    query_pad = query_pad.reshape(per_dev, CH, heads_local, HD)
    score_scale = HD ** (-0.5)
    scores = (
        jnp.einsum("swhd,skhd->shwk", query_pad, key_heads, preferred_element_type=jnp.float32)
        * score_scale
    )
    row_max = jnp.max(scores, axis=-1, keepdims=True)
    expo = jnp.exp(scores - row_max)
    probs = expo / jnp.sum(expo, axis=-1, keepdims=True)
    weights_bf = probs.astype(jnp.bfloat16)
    window_out = jnp.einsum(
        "shwk,skhd->swhd", weights_bf, val_heads, preferred_element_type=jnp.float32
    )
    window_rows = window_out.astype(jnp.bfloat16).reshape(tok_rows, hd_local)
    attention = jnp.concatenate(
        [jnp.zeros((CH - 1, hd_local), jnp.bfloat16), window_rows[: tok_rows - (CH - 1)]], axis=0
    )
    partial_value = lax.dot_general(
        attention, out_weight, (((1,), (1,)), ((), ())), preferred_element_type=jnp.float32
    )
    return lax.psum_scatter(partial_value, "head", scatter_dimension=1, tiled=True).astype(
        jnp.bfloat16
    )


def solution(mesh):
    sizes = dict(mesh.shape)
    small = sizes["shard"] == NZ * PLANE and sizes["head"] == 2
    return jax.shard_map(
        local_small if small else local_general,
        mesh=mesh,
        in_specs=(
            P("shard", "head"),
            P("shard", "head"),
            P("shard", "head"),
            P(None, "head"),
            P("shard", "head", None),
            P(),
            P(),
        ),
        out_specs=P("shard", "head"),
        check_vma=False,
    )
```

```python
import jax
import jax.numpy as jnp
from jax import lax
from jax.experimental import pallas as pl
from jax.experimental.pallas import tpu as pltpu
from jax.sharding import PartitionSpec as P

HD = 128
CH = 64
KNB = 2
NZ, NY, NX = 4, 2, 2
PLANE = NY * NX
EDGE = 16
Z_PARTS = 4
E_PARTS = (2, 2, 2, 2)
OUT_TILE = 1024
MESH = pl.DeviceIdType.MESH
VMEM_LIMIT = 60 * 1024 * 1024
NT = (((1,), (1,)), ((), ()))


def shifted(shard, dy, dx):
    z, y, x = shard // PLANE, (shard // NX) % NY, shard % NX
    return z * PLANE + ((y + dy) % NY) * NX + (x + dx) % NX


def fused_kernel(
    near_ref, place_ref, q_ref, kw_ref, vw_ref, ow_ref, db_ref,
    out_ref,
    w, sets, e_out, e_in, pass_out, pass_in, kv, q_pad, att, ow_own, ow_other,
    s_send, s_recv, a_send, a_recv, f_send, f_recv, z_send, p_send, g_send, c_send, w_recv, o_sem,
    b_send, b_recv, n_send, t_send, t_recv, l_sem, z_ready,
):
    s = lax.axis_index("shard")
    h = lax.axis_index("head")
    z, y, x = s // PLANE, (s // NX) % NY, s % NX
    near_x = s + 1 - 2 * x
    near_y = s + NX * (1 - 2 * y)
    n = NZ * PLANE
    groups, _, width = q_ref.shape
    blk, half, de = db_ref.shape
    feats = ow_own.shape[0]
    picks = near_ref.shape[0] * near_ref.shape[1] // n
    is_end = (z == 0) | (z == NZ - 1)
    near, mid, far = jnp.where(z == 1, 0, NZ - 1), NZ - 1 - z, jnp.where(z == 1, NZ - 1, 0)

    barrier = pltpu.get_barrier_semaphore()

    def greet(to, head):
        pl.semaphore_signal(barrier, inc=1, device_id=(to, head), device_id_type=MESH)

    for j in range(1, PLANE):
        greet(shifted(s, j // NX, j % NX), h)
    greet(s, 1 - h)

    @pl.when((z == 0) | (z == 1))
    def _():
        greet(s + PLANE, h)

    @pl.when((z == 2) | (z == 3))
    def _():
        greet(s - PLANE, h)

    loads = [
        pltpu.make_async_copy(kw_ref, w.at[0, s], l_sem.at[0]),
        pltpu.make_async_copy(vw_ref, w.at[1, s], l_sem.at[1]),
        pltpu.make_async_copy(db_ref, sets.at[z], l_sem.at[2]),
        pltpu.make_async_copy(q_ref, q_pad, l_sem.at[3]),
        pltpu.make_async_copy(ow_ref.at[pl.ds(h * feats, feats)], ow_own, l_sem.at[4]),
    ]
    for load in loads:
        load.start()

    @pl.when(is_end)
    def _():
        pl.semaphore_wait(barrier, PLANE)

    @pl.when(~is_end)
    def _():
        pl.semaphore_wait(barrier, PLANE + 2)

    @pl.when(z == 1)
    def _():
        pl.semaphore_signal(z_ready, inc=1, device_id=(s - PLANE, h), device_id_type=MESH)

    @pl.when(z == 2)
    def _():
        pl.semaphore_signal(z_ready, inc=1, device_id=(s + PLANE, h), device_id_type=MESH)

    def weight_copy(kind, chunk, to, sem, own=False):
        return pltpu.make_async_remote_copy(
            src_ref=(kw_ref, vw_ref)[kind] if own else w.at[kind, chunk], dst_ref=w.at[kind, chunk],
            send_sem=sem, recv_sem=w_recv.at[kind, chunk], device_id=(to, h), device_id_type=MESH)

    def column(zz):
        return zz * PLANE + y * NX + x

    def up_copy(kind, zz, own=False):
        return weight_copy(kind, column(zz), s + PLANE, z_send.at[0, kind, zz], own)

    def down_copy(kind, zz, own=False):
        return weight_copy(kind, column(zz), s - PLANE, z_send.at[1, kind, zz], own)

    def x_copy(kind, zz, own=False):
        return weight_copy(kind, column(zz), near_x, p_send.at[0, kind, zz], own)

    def y_copy(kind, zz, own=False):
        return weight_copy(kind, column(zz), near_y, p_send.at[1, kind, zz], own)

    def diag_k(zz):
        return weight_copy(0, zz * PLANE + y * NX + 1 - x, near_y, g_send.at[0, zz])

    def diag_v(zz):
        return weight_copy(1, zz * PLANE + (1 - y) * NX + x, near_x, g_send.at[1, zz])

    columns = (y * NX + 1 - x, (1 - y) * NX + x, (1 - y) * NX + 1 - x)

    def across(kind, c):
        to = jnp.where(z == 0, s + PLANE, s - PLANE)
        return weight_copy(kind, z * PLANE + columns[c], to, c_send.at[kind, c])

    def arrive(kind, chunk):
        weight_copy(kind, chunk, near_x, z_send.at[0, 0, 0]).wait_recv()

    z_rows = half // Z_PARTS

    def set_copy(way, zz, r):
        part = sets.at[zz, :, pl.ds(r * z_rows, z_rows)]
        return pltpu.make_async_remote_copy(
            src_ref=part, dst_ref=part, send_sem=s_send.at[way, zz, r], recv_sem=s_recv.at[zz, r],
            device_id=(s + PLANE - 2 * PLANE * way, h), device_id_type=MESH)

    def enc_copy(zz, j, r, parts):
        d = zz * PLANE + j
        rows = pl.ds(r * (half // parts), half // parts)
        return pltpu.make_async_remote_copy(
            src_ref=e_out.at[d, rows], dst_ref=e_in.at[d, h, rows], send_sem=a_send.at[d, r],
            recv_sem=a_recv.at[d, r], device_id=(shifted(s, j // NX, j % NX), h),
            device_id_type=MESH)

    def half_copy(d, r, parts, head):
        piece = e_in.at[d, head, pl.ds(r * (half // parts), half // parts)]
        return pltpu.make_async_remote_copy(
            src_ref=piece, dst_ref=piece, send_sem=f_send.at[d, r], recv_sem=f_recv.at[d, r],
            device_id=(s, 1 - h), device_id_type=MESH)

    def pass_copy(j, r, parts):
        rows = pl.ds(r * (half // parts), half // parts)
        return pltpu.make_async_remote_copy(
            src_ref=pass_out.at[j, rows], dst_ref=pass_in.at[j, rows], send_sem=b_send.at[j, r],
            recv_sem=b_recv.at[j, r], device_id=(shifted(s, j // NX, j % NX), h),
            device_id_type=MESH)

    def last_copy(j, r, parts):
        rows = pl.ds(r * (half // parts), half // parts)
        d = far * PLANE + j
        return pltpu.make_async_remote_copy(
            src_ref=(pass_in if j else pass_out).at[j, rows], dst_ref=e_in.at[d, h, rows],
            send_sem=n_send.at[j, r], recv_sem=a_recv.at[d, r],
            device_id=(jnp.where(z == 1, s - PLANE, s + PLANE), h), device_id_type=MESH)

    def out_copy():
        return pltpu.make_async_remote_copy(
            src_ref=ow_ref.at[pl.ds((1 - h) * feats, feats)], dst_ref=ow_other,
            send_sem=o_sem.at[0], recv_sem=o_sem.at[1], device_id=(s, 1 - h),
            device_id_type=MESH)

    def swap(c):
        rows = pl.ds(c * CH, CH)
        return pltpu.make_async_remote_copy(
            src_ref=att.at[0, rows], dst_ref=att.at[1, rows], send_sem=t_send.at[c],
            recv_sem=t_recv.at[c], device_id=(s, 1 - h), device_id_type=MESH)

    def pick(to, i):
        return place_ref[near_ref[i % KNB, to * (picks // KNB) + i // KNB]]

    def find(j):
        to = shifted(s, j // NX, j % NX)
        found = [jnp.int32(0)] * NZ
        for i in range(picks):
            slot = pick(to, i)
            owner, block = slot // blk, slot % blk
            found = [
                got + jnp.where(owner == column(zz), block, 0) for zz, got in enumerate(found)]
        return found

    def find_last(j):
        to = near * PLANE + shifted(s, j // NX, j % NX) % PLANE
        found = jnp.int32(0)
        for i in range(picks):
            slot = pick(to, i)
            found += jnp.where(slot // blk == column(far), slot % blk, 0)
        return found

    def slot_of(i):
        own = pick(s, i) // blk
        return own // PLANE * PLANE + (y + own // NX) % NY * NX + (x + own) % NX

    def onward(zz, up, down):
        @pl.when((zz <= z) & (z < NZ - 1))
        def _():
            up()

        @pl.when((zz >= z) & (z > 0))
        def _():
            down()

    def send_on(kind, zz, own=False):
        onward(
            zz, lambda: up_copy(kind, zz, own).start(), lambda: down_copy(kind, zz, own).start())

    def send_set(zz, parts):
        for r in parts:
            onward(zz, lambda: set_copy(0, zz, r).start(), lambda: set_copy(1, zz, r).start())

    def weights_in(kind, zz, share=True):
        arrive(kind, column(zz))
        send_on(kind, zz)
        if share:
            x_copy(kind, zz).start()
            y_copy(kind, zz).start()

    def turn_k(zz):
        arrive(0, zz * PLANE + columns[0])
        diag_k(zz).start()

    def turn_v(zz):
        arrive(1, zz * PLANE + columns[1])
        diag_v(zz).start()

    def rest_in(zz):
        arrive(1, zz * PLANE + columns[0])
        arrive(0, zz * PLANE + columns[1])
        for kind in range(2):
            arrive(kind, zz * PLANE + columns[2])

    def set_in(zz, parts):
        for r in parts:
            set_copy(0, zz, r).wait_recv()
            send_set(zz, [r])

    def take(zz, block, rows):
        got = sets[zz, 0, rows]
        for b in range(1, blk):
            got = lax.select(block == b, sets[zz, b, rows], got)
        return got

    def pass_last(r):
        parts = E_PARTS[-1]
        rows = pl.ds(r * (half // parts), half // parts)
        for j in range(1, PLANE):
            pass_out[j, rows] = take(far, last_blocks[j], rows)
            pass_copy(j, r, parts).start()
        pass_out[0, rows] = take(far, last_blocks[0], rows)
        last_copy(0, r, parts).start()

    def forward_last(r):
        for j in range(1, PLANE):
            pass_copy(j, r, E_PARTS[-1]).wait_recv()
            last_copy(j, r, E_PARTS[-1]).start()

    def spread(zz, r, parts):
        rows = pl.ds(r * (half // parts), half // parts)

        def taken(j):
            return take(zz, chosen(zz, j), rows)

        for j in range(1, PLANE):
            e_out[zz * PLANE + j, rows] = taken(j)
            enc_copy(zz, j, r, parts).start()
        e_in[zz * PLANE, h, rows] = taken(0)
        half_copy(zz * PLANE, r, parts, h).start()

    def spread_in(p, r):
        zz, parts = plane_at(p), E_PARTS[p]
        for part in range(r * Z_PARTS // parts, (r + 1) * Z_PARTS // parts):
            set_copy(0, zz, part).wait_recv()
        spread(zz, r, parts)

    for kind in range(2):
        @pl.when(~is_end)
        def _():
            send_on(kind, z, own=True)
        x_copy(kind, z, own=True).start()
        y_copy(kind, z, own=True).start()
    for load in loads[:3]:
        load.wait()

    out_copy().start()
    blocks = [find(j) for j in range(PLANE)]
    last_blocks = [find_last(j) for j in range(PLANE)]

    def chosen(zz, j):
        return sum(jnp.where(zz == i, got, 0) for i, got in enumerate(blocks[j]))

    def plane_at(p):
        at_end = jnp.where(z == 0, p, NZ - 1 - p)
        between = jnp.where(p == 0, z, jnp.where(p == 1, mid, jnp.where(p == 2, near, far)))
        return jnp.where(is_end, at_end, between)

    @pl.when(is_end)
    def _():
        one, two, three = plane_at(1), plane_at(2), plane_at(3)
        turn_k(z)
        turn_v(z)
        for r in range(E_PARTS[0]):
            spread(z, r, E_PARTS[0])
        pl.semaphore_wait(z_ready, 1)
        for kind in range(2):
            send_on(kind, z, own=True)
        across(0, 0).start()
        across(1, 1).start()
        rest_in(z)
        across(1, 0).start()
        across(0, 1).start()
        for kind in range(2):
            across(kind, 2).start()
        send_set(z, range(Z_PARTS))
        weights_in(0, one)
        weights_in(1, one)
        weights_in(0, two)
        turn_k(one)
        weights_in(1, two)
        turn_v(one)
        weights_in(0, three)
        turn_k(two)
        weights_in(1, three)
        turn_v(two)
        turn_k(three)
        spread_in(1, 0)
        turn_v(three)
        spread_in(1, 1)
        for k in (one, two, three):
            rest_in(k)

    @pl.when(~is_end)
    def _():
        weights_in(0, mid)
        turn_k(z)
        weights_in(0, near, share=False)
        weights_in(1, mid)
        weights_in(1, near, share=False)
        send_set(z, [0])
        turn_v(z)
        weights_in(0, far)
        turn_k(mid)
        weights_in(1, far)
        send_set(z, range(1, Z_PARTS))
        turn_v(mid)
        set_in(mid, [0, 1])
        turn_k(far)
        set_in(mid, [2, 3])
        turn_v(far)
        for zz, r in ((z, 0), (z, 1), (mid, 0)):
            spread(zz, r, 2)

    def far_in(parts):
        for r in parts:
            set_copy(0, far, r).wait_recv()

    def weights_complete():
        for zz in (z, mid, far):
            rest_in(zz)
        for kind in range(2):
            for c in range(2):
                if (kind, c) in ((0, 0), (1, 1)):
                    arrive(kind, near * PLANE + columns[c])
        rest_in(near)

    def weights_sent():
        for zz in range(NZ):
            for kind in range(2):
                onward(zz, lambda: up_copy(kind, zz).wait_send(), lambda: down_copy(kind, zz).wait_send())

            @pl.when(is_end | (near != zz))
            def _():
                for kind in range(2):
                    x_copy(kind, zz).wait_send()
                    y_copy(kind, zz).wait_send()
                diag_k(zz).wait_send()
                diag_v(zz).wait_send()

        @pl.when(is_end)
        def _():
            for kind in range(2):
                for c in range(PLANE - 1):
                    across(kind, c).wait_send()

    def pass_halves(p, r):
        zz = plane_at(p)

        def one(j):
            enc_copy(zz, j, r, E_PARTS[p]).wait_recv()
            half_copy(zz * PLANE + j, r, E_PARTS[p], h).start()

        if p == NZ - 1:
            @pl.when(is_end)
            def _():
                one(0)
        for j in range(1, PLANE):
            one(j)

    def halves_in(p, r):
        for j in range(PLANE):
            half_copy(plane_at(p) * PLANE + j, r, E_PARTS[p], 1 - h).wait_recv()

    def project(zz, kind, first, count):
        slab = pl.ds(zz * PLANE, PLANE)
        rows = pl.ds(first, count)
        enc = e_in[slab, :, rows].reshape(PLANE * 2 * count, de)
        got = jnp.dot(enc, w[kind].reshape(de, width), preferred_element_type=jnp.float32)
        kv[kind, slab, :, rows] = got.astype(jnp.bfloat16).reshape(PLANE, 2, count, width)

    loads[3].wait()

    def taken_in(p, parts=None):
        parts = range(E_PARTS[p]) if parts is None else parts
        for r in parts:
            pass_halves(p, r)
        for r in parts:
            halves_in(p, r)

    def before(step):
        end_pieces = {1: [(2, 0)], 4: [(2, 1)]}

        @pl.when(is_end)
        def _():
            for p, r in end_pieces.get(step, []):
                spread_in(p, r)

        @pl.when(~is_end)
        def _():
            if step == 0:
                set_in(near, [0, 1])
                far_in([0])
                set_in(near, [2])
                far_in([1])
                pass_last(0)
                spread(mid, 1, 2)
                weights_complete()
            if step == 1:
                set_in(near, [3])
                spread(near, 0, 2)
            if step == 2:
                far_in([2, 3])
                pass_last(1)
                spread(near, 1, 2)
                forward_last(0)
            if step == 3:
                forward_last(1)
            if step == 4:
                for r in range(2):
                    spread(far, r, 2)

        if step in (0, 2, 4):
            taken_in(step // 2)
        if step == 3:
            weights_sent()

    @pl.loop(0, 2 * (NZ - 1))
    def _(step):
        for k in range(2 * (NZ - 1)):
            @pl.when(step == k)
            def _():
                before(k)
        project(plane_at(step // 2), step % 2, 0, half)

    @pl.loop(0, 2)
    def _(side):
        for k in range(2):
            @pl.when(side == k)
            def _():
                taken_in(NZ - 1, range(k * E_PARTS[-1] // 2, (k + 1) * E_PARTS[-1] // 2))

        @pl.loop(0, 2)
        def _(kind):
            project(plane_at(NZ - 1), kind, pl.multiple_of(side * (half // 2), half // 2), half // 2)

    scale = HD ** -0.5

    def attend(c, full):
        one, two = slot_of(KNB * c), slot_of(KNB * c + 1)
        last = lax.broadcasted_iota(jnp.int32, (EDGE, HD), 0) == EDGE - 1
        edge = pl.ds(pl.multiple_of(c * CH + CH - EDGE, EDGE), EDGE)
        batch = 8

        def held(kind, cols):
            return jnp.concatenate(
                [kv[kind, one, :, :, cols].reshape(2 * half, HD),
                 kv[kind, two, :, :, cols].reshape(2 * half, HD)], axis=0)

        for first in range(0, width // HD, batch):
            spans = [slice(i * HD, (i + 1) * HD) for i in range(first, first + batch)]
            scores = []
            for cols in spans:
                q = q_pad[c, CH - EDGE:, cols]
                if full:
                    q = jnp.concatenate([q, q_pad[c + 1, :, cols]], axis=0)
                scores.append(
                    lax.dot_general(q, held(0, cols), NT, preferred_element_type=jnp.float32) * scale)
            tops = [jnp.max(score, axis=1, keepdims=True) for score in scores]
            expos = [jnp.exp(score - top) for score, top in zip(scores, tops)]
            sums = [jnp.sum(expo, axis=1, keepdims=True) for expo in expos]
            weights = [(expo / total).astype(jnp.bfloat16) for expo, total in zip(expos, sums)]
            outs = [
                jnp.dot(weight, held(1, cols), preferred_element_type=jnp.float32)
                for cols, weight in zip(spans, weights)]
            for cols, got in zip(spans, outs):
                old = att[0, edge, cols].astype(jnp.float32)
                att[0, edge, cols] = jnp.where(last, got[:EDGE], old).astype(jnp.bfloat16)
                if full:
                    att[0, pl.ds(pl.multiple_of(c * CH + CH, CH), CH), cols] = (
                        got[EDGE:].astype(jnp.bfloat16))

    att[0, 0:CH] = jnp.zeros((CH, width), jnp.bfloat16)

    @pl.loop(0, groups - 1)
    def _(c):
        attend(c, True)
        swap(c).start()

    attend(groups - 1, False)
    swap(groups - 1).start()

    def mix(t, side, held):
        rows = pl.ds(pl.multiple_of(t * OUT_TILE, OUT_TILE), OUT_TILE)
        return lax.dot_general(att[side], held[rows], NT, preferred_element_type=jnp.float32)

    loads[4].wait()
    mine = mix(0, 0, ow_own)
    out_copy().wait()
    for c in range(groups):
        swap(c).wait_recv()
    out_ref[:, 0:OUT_TILE] = (mine + mix(0, 1, ow_other)).astype(jnp.bfloat16)

    @pl.loop(1, feats // OUT_TILE)
    def _(t):
        got = mix(t, 0, ow_own) + mix(t, 1, ow_other)
        out_ref[:, pl.ds(pl.multiple_of(t * OUT_TILE, OUT_TILE), OUT_TILE)] = got.astype(jnp.bfloat16)

    for zz in range(NZ):
        for r in range(Z_PARTS):
            @pl.when(is_end | (zz != far))
            def _():
                onward(zz, lambda: set_copy(0, zz, r).wait_send(), lambda: set_copy(1, zz, r).wait_send())
    for p in range(NZ):
        zz = plane_at(p)
        for j in range(PLANE):
            for r in range(E_PARTS[p]):
                if j:
                    @pl.when(~is_end | (p < NZ - 1))
                    def _():
                        enc_copy(zz, j, r, E_PARTS[p]).wait_send()
                half_copy(zz * PLANE + j, r, E_PARTS[p], h).wait_send()

    @pl.when(~is_end)
    def _():
        for j in range(PLANE):
            for r in range(E_PARTS[-1]):
                if j:
                    pass_copy(j, r, E_PARTS[-1]).wait_send()
                last_copy(j, r, E_PARTS[-1]).wait_send()

    for c in range(groups):
        swap(c).wait_send()


def local_small(queries, key_weight, value_weight, out_weight, database, neighbours, placement):
    n = NZ * PLANE
    tok, width = queries.shape
    blk, half, de = database.shape
    feats = out_weight.shape[0] // 2
    groups = tok // CH
    sm = pl.BlockSpec(memory_space=pltpu.SMEM)
    hbm = pl.BlockSpec(memory_space=pl.ANY)
    dma = pltpu.SemaphoreType.DMA
    bf16 = jnp.bfloat16
    return pl.pallas_call(
        fused_kernel,
        out_shape=pltpu.VMEM((tok, feats), bf16),
        in_specs=[sm, sm] + [hbm] * 5,
        out_specs=pl.BlockSpec(memory_space=pltpu.VMEM),
        scratch_shapes=[
            pltpu.VMEM((2, n) + key_weight.shape, bf16),
            pltpu.VMEM((NZ,) + database.shape, bf16),
            pltpu.VMEM((n, half, de), bf16),
            pltpu.VMEM((n, 2, half, de), bf16),
            pltpu.VMEM((PLANE, half, de), bf16),
            pltpu.VMEM((PLANE, half, de), bf16),
            pltpu.VMEM((2, n, 2, half, width), bf16),
            pltpu.VMEM((groups, CH, width), bf16),
            pltpu.VMEM((2, tok, width), bf16),
            pltpu.VMEM((feats, width), bf16),
            pltpu.VMEM((feats, width), bf16),
            dma((2, NZ, Z_PARTS)), dma((NZ, Z_PARTS)), dma((n, max(E_PARTS))), dma((n, max(E_PARTS))),
            dma((n, max(E_PARTS))), dma((n, max(E_PARTS))), dma((2, 2, NZ)), dma((2, 2, NZ)), dma((2, NZ)),
            dma((2, PLANE - 1)), dma((2, n)), dma((2,)),
            *[dma((PLANE, max(E_PARTS)))] * 3, dma((groups,)), dma((groups,)), dma((5,)),
            pltpu.SemaphoreType.REGULAR,
        ],
        compiler_params=pltpu.CompilerParams(
            collective_id=0, has_side_effects=True, vmem_limit_bytes=VMEM_LIMIT),
    )(neighbours.T, placement, queries.reshape(groups, CH, width), key_weight, value_weight, out_weight, database)


def local_general(queries, key_weight, value_weight, out_weight, database, neighbours, placement):
    shard_count = lax.axis_size("shard")
    shard_self = lax.axis_index("shard")
    tok_rows = queries.shape[0]
    hd_local = queries.shape[1]
    heads_local = hd_local // HD
    per_dev = tok_rows // CH
    blk_local = database.shape[0]
    slots = placement[neighbours]
    needed = slots.reshape(shard_count, per_dev * KNB)
    owners = needed // blk_local
    matches = owners == shard_self
    hits = jnp.any(matches, axis=1)
    which = jnp.sum(jnp.where(matches, needed % blk_local, 0), axis=1)
    outgoing = jnp.zeros((shard_count,) + database.shape[1:], jnp.bfloat16)
    for b in range(blk_local):
        taken = (hits & (which == b))[:, None, None]
        outgoing = jnp.where(taken, database[b][None], outgoing)
    arrived = lax.all_to_all(outgoing, "shard", split_axis=0, concat_axis=0, tiled=True)
    own_need = lax.dynamic_slice_in_dim(needed, shard_self, 1, 0)[0]
    half_rows = jnp.concatenate(
        [
            lax.dynamic_slice_in_dim(arrived, own_need[i] // blk_local, 1, 0)
            for i in range(per_dev * KNB)
        ],
        axis=0,
    )
    encoded = lax.all_gather(half_rows, "head", axis=1, tiled=True)
    key_rows, val_rows = (
        lax.all_gather(key_weight, "shard", axis=0, tiled=True),
        lax.all_gather(value_weight, "shard", axis=0, tiled=True),
    )
    key_block = jnp.einsum(
        "brd,de->bre", encoded, key_rows, preferred_element_type=jnp.float32
    ).astype(jnp.bfloat16)
    val_block = jnp.einsum(
        "brd,de->bre", encoded, val_rows, preferred_element_type=jnp.float32
    ).astype(jnp.bfloat16)
    neighbour_len = encoded.shape[1]
    key_heads = key_block.reshape(per_dev, KNB * neighbour_len, heads_local, HD)
    val_heads = val_block.reshape(per_dev, KNB * neighbour_len, heads_local, HD)
    query_pad = jnp.concatenate(
        [queries[CH - 1 :], jnp.zeros((CH - 1, hd_local), jnp.bfloat16)], axis=0
    )
    query_pad = query_pad.reshape(per_dev, CH, heads_local, HD)
    score_scale = HD ** (-0.5)
    scores = (
        jnp.einsum("swhd,skhd->shwk", query_pad, key_heads, preferred_element_type=jnp.float32)
        * score_scale
    )
    row_max = jnp.max(scores, axis=-1, keepdims=True)
    expo = jnp.exp(scores - row_max)
    probs = expo / jnp.sum(expo, axis=-1, keepdims=True)
    weights_bf = probs.astype(jnp.bfloat16)
    window_out = jnp.einsum(
        "shwk,skhd->swhd", weights_bf, val_heads, preferred_element_type=jnp.float32
    )
    window_rows = window_out.astype(jnp.bfloat16).reshape(tok_rows, hd_local)
    attention = jnp.concatenate(
        [jnp.zeros((CH - 1, hd_local), jnp.bfloat16), window_rows[: tok_rows - (CH - 1)]], axis=0
    )
    partial_value = lax.dot_general(
        attention, out_weight, (((1,), (1,)), ((), ())), preferred_element_type=jnp.float32
    )
    return lax.psum_scatter(partial_value, "head", scatter_dimension=1, tiled=True).astype(
        jnp.bfloat16
    )


def solution(mesh):
    sizes = dict(mesh.shape)
    small = sizes["shard"] == NZ * PLANE and sizes["head"] == 2
    return jax.shard_map(
        local_small if small else local_general,
        mesh=mesh,
        in_specs=(
            P("shard", "head"),
            P("shard", "head"),
            P("shard", "head"),
            P(None, "head"),
            P("shard", "head", None),
            P(),
            P(),
        ),
        out_specs=P("shard", "head"),
        check_vma=False,
    )
```

```python
import jax
import jax.numpy as jnp
from jax import lax
from jax.experimental import pallas as pl
from jax.experimental.pallas import tpu as pltpu
from jax.sharding import PartitionSpec as P

HD = 128
CH = 64
KNB = 2
NZ, NY, NX = 4, 2, 2
PLANE = NY * NX
EDGE = 16
Z_PARTS = 4
E_PARTS = (2, 2, 2, 2)
OUT_TILE = 1024
MESH = pl.DeviceIdType.MESH
VMEM_LIMIT = 60 * 1024 * 1024
NT = (((1,), (1,)), ((), ()))


def shifted(shard, dy, dx):
    z, y, x = shard // PLANE, (shard // NX) % NY, shard % NX
    return z * PLANE + ((y + dy) % NY) * NX + (x + dx) % NX


def fused_kernel(
    near_ref, place_ref, q_ref, kw_ref, vw_ref, ow_ref, db_ref,
    out_ref,
    w, sets, e_out, e_in, pass_out, pass_in, kv, q_pad, att, ow_own, ow_other,
    s_send, s_recv, a_send, a_recv, f_send, f_recv, z_send, p_send, g_send, c_send, w_recv, o_sem,
    b_send, b_recv, n_send, t_send, t_recv, l_sem, z_ready,
):
    s = lax.axis_index("shard")
    h = lax.axis_index("head")
    z, y, x = s // PLANE, (s // NX) % NY, s % NX
    near_x = s + 1 - 2 * x
    near_y = s + NX * (1 - 2 * y)
    n = NZ * PLANE
    groups, _, width = q_ref.shape
    blk, half, de = db_ref.shape
    feats = ow_own.shape[0]
    picks = near_ref.shape[0] * near_ref.shape[1] // n
    is_end = (z == 0) | (z == NZ - 1)
    near, mid, far = jnp.where(z == 1, 0, NZ - 1), NZ - 1 - z, jnp.where(z == 1, NZ - 1, 0)

    barrier = pltpu.get_barrier_semaphore()

    def greet(to, head):
        pl.semaphore_signal(barrier, inc=1, device_id=(to, head), device_id_type=MESH)

    for j in range(1, PLANE):
        greet(shifted(s, j // NX, j % NX), h)
    greet(s, 1 - h)

    @pl.when((z == 0) | (z == 1))
    def _():
        greet(s + PLANE, h)

    @pl.when((z == 2) | (z == 3))
    def _():
        greet(s - PLANE, h)

    loads = [
        pltpu.make_async_copy(kw_ref, w.at[0, s], l_sem.at[0]),
        pltpu.make_async_copy(vw_ref, w.at[1, s], l_sem.at[1]),
        pltpu.make_async_copy(db_ref, sets.at[z], l_sem.at[2]),
        pltpu.make_async_copy(q_ref, q_pad, l_sem.at[3]),
        pltpu.make_async_copy(ow_ref.at[pl.ds(h * feats, feats)], ow_own, l_sem.at[4]),
    ]
    for load in loads:
        load.start()

    @pl.when(is_end)
    def _():
        pl.semaphore_wait(barrier, PLANE)

    @pl.when(~is_end)
    def _():
        pl.semaphore_wait(barrier, PLANE + 2)

    @pl.when(z == 1)
    def _():
        pl.semaphore_signal(z_ready, inc=1, device_id=(s - PLANE, h), device_id_type=MESH)

    @pl.when(z == 2)
    def _():
        pl.semaphore_signal(z_ready, inc=1, device_id=(s + PLANE, h), device_id_type=MESH)

    def weight_copy(kind, chunk, to, sem, own=False):
        return pltpu.make_async_remote_copy(
            src_ref=(kw_ref, vw_ref)[kind] if own else w.at[kind, chunk], dst_ref=w.at[kind, chunk],
            send_sem=sem, recv_sem=w_recv.at[kind, chunk], device_id=(to, h), device_id_type=MESH)

    def column(zz):
        return zz * PLANE + y * NX + x

    def up_copy(kind, zz, own=False):
        return weight_copy(kind, column(zz), s + PLANE, z_send.at[0, kind, zz], own)

    def down_copy(kind, zz, own=False):
        return weight_copy(kind, column(zz), s - PLANE, z_send.at[1, kind, zz], own)

    def x_copy(kind, zz, own=False):
        return weight_copy(kind, column(zz), near_x, p_send.at[0, kind, zz], own)

    def y_copy(kind, zz, own=False):
        return weight_copy(kind, column(zz), near_y, p_send.at[1, kind, zz], own)

    def diag_k(zz):
        return weight_copy(0, zz * PLANE + y * NX + 1 - x, near_y, g_send.at[0, zz])

    def diag_v(zz):
        return weight_copy(1, zz * PLANE + (1 - y) * NX + x, near_x, g_send.at[1, zz])

    columns = (y * NX + 1 - x, (1 - y) * NX + x, (1 - y) * NX + 1 - x)

    def across(kind, c):
        to = jnp.where(z == 0, s + PLANE, s - PLANE)
        return weight_copy(kind, z * PLANE + columns[c], to, c_send.at[kind, c])

    def arrive(kind, chunk):
        weight_copy(kind, chunk, near_x, z_send.at[0, 0, 0]).wait_recv()

    z_rows = half // Z_PARTS

    def set_copy(way, zz, r):
        part = sets.at[zz, :, pl.ds(r * z_rows, z_rows)]
        return pltpu.make_async_remote_copy(
            src_ref=part, dst_ref=part, send_sem=s_send.at[way, zz, r], recv_sem=s_recv.at[zz, r],
            device_id=(s + PLANE - 2 * PLANE * way, h), device_id_type=MESH)

    def enc_copy(zz, j, r, parts):
        d = zz * PLANE + j
        rows = pl.ds(r * (half // parts), half // parts)
        return pltpu.make_async_remote_copy(
            src_ref=e_out.at[d, rows], dst_ref=e_in.at[d, h, rows], send_sem=a_send.at[d, r],
            recv_sem=a_recv.at[d, r], device_id=(shifted(s, j // NX, j % NX), h),
            device_id_type=MESH)

    def half_copy(d, r, parts, head):
        piece = e_in.at[d, head, pl.ds(r * (half // parts), half // parts)]
        return pltpu.make_async_remote_copy(
            src_ref=piece, dst_ref=piece, send_sem=f_send.at[d, r], recv_sem=f_recv.at[d, r],
            device_id=(s, 1 - h), device_id_type=MESH)

    def pass_copy(j, r, parts):
        rows = pl.ds(r * (half // parts), half // parts)
        return pltpu.make_async_remote_copy(
            src_ref=pass_out.at[j, rows], dst_ref=pass_in.at[j, rows], send_sem=b_send.at[j, r],
            recv_sem=b_recv.at[j, r], device_id=(shifted(s, j // NX, j % NX), h),
            device_id_type=MESH)

    def last_copy(j, r, parts):
        rows = pl.ds(r * (half // parts), half // parts)
        d = far * PLANE + j
        return pltpu.make_async_remote_copy(
            src_ref=(pass_in if j else pass_out).at[j, rows], dst_ref=e_in.at[d, h, rows],
            send_sem=n_send.at[j, r], recv_sem=a_recv.at[d, r],
            device_id=(jnp.where(z == 1, s - PLANE, s + PLANE), h), device_id_type=MESH)

    def out_copy():
        return pltpu.make_async_remote_copy(
            src_ref=ow_ref.at[pl.ds((1 - h) * feats, feats)], dst_ref=ow_other,
            send_sem=o_sem.at[0], recv_sem=o_sem.at[1], device_id=(s, 1 - h),
            device_id_type=MESH)

    def swap(c):
        rows = pl.ds(c * CH, CH)
        return pltpu.make_async_remote_copy(
            src_ref=att.at[0, rows], dst_ref=att.at[1, rows], send_sem=t_send.at[c],
            recv_sem=t_recv.at[c], device_id=(s, 1 - h), device_id_type=MESH)

    def pick(to, i):
        return place_ref[near_ref[i % KNB, to * (picks // KNB) + i // KNB]]

    def find(j):
        to = shifted(s, j // NX, j % NX)
        found = [jnp.int32(0)] * NZ
        for i in range(picks):
            slot = pick(to, i)
            owner, block = slot // blk, slot % blk
            found = [
                got + jnp.where(owner == column(zz), block, 0) for zz, got in enumerate(found)]
        return found

    def find_last(j):
        to = near * PLANE + shifted(s, j // NX, j % NX) % PLANE
        found = jnp.int32(0)
        for i in range(picks):
            slot = pick(to, i)
            found += jnp.where(slot // blk == column(far), slot % blk, 0)
        return found

    def slot_of(i):
        own = pick(s, i) // blk
        return own // PLANE * PLANE + (y + own // NX) % NY * NX + (x + own) % NX

    def onward(zz, up, down):
        @pl.when((zz <= z) & (z < NZ - 1))
        def _():
            up()

        @pl.when((zz >= z) & (z > 0))
        def _():
            down()

    def send_on(kind, zz, own=False):
        onward(
            zz, lambda: up_copy(kind, zz, own).start(), lambda: down_copy(kind, zz, own).start())

    def send_set(zz, parts):
        for r in parts:
            onward(zz, lambda: set_copy(0, zz, r).start(), lambda: set_copy(1, zz, r).start())

    def weights_in(kind, zz, share=True):
        arrive(kind, column(zz))
        send_on(kind, zz)
        if share:
            x_copy(kind, zz).start()
            y_copy(kind, zz).start()

    def turn_k(zz):
        arrive(0, zz * PLANE + columns[0])
        diag_k(zz).start()

    def turn_v(zz):
        arrive(1, zz * PLANE + columns[1])
        diag_v(zz).start()

    def rest_in(zz):
        arrive(1, zz * PLANE + columns[0])
        arrive(0, zz * PLANE + columns[1])
        for kind in range(2):
            arrive(kind, zz * PLANE + columns[2])

    def set_in(zz, parts):
        for r in parts:
            set_copy(0, zz, r).wait_recv()
            send_set(zz, [r])

    def take(zz, block, rows):
        got = sets[zz, 0, rows]
        for b in range(1, blk):
            got = lax.select(block == b, sets[zz, b, rows], got)
        return got

    def pass_last(r):
        parts = E_PARTS[-1]
        rows = pl.ds(r * (half // parts), half // parts)
        for j in range(1, PLANE):
            pass_out[j, rows] = take(far, last_blocks[j], rows)
            pass_copy(j, r, parts).start()
        pass_out[0, rows] = take(far, last_blocks[0], rows)
        last_copy(0, r, parts).start()

    def forward_last(r):
        for j in range(1, PLANE):
            pass_copy(j, r, E_PARTS[-1]).wait_recv()
            last_copy(j, r, E_PARTS[-1]).start()

    def spread(zz, r, parts):
        rows = pl.ds(r * (half // parts), half // parts)

        def taken(j):
            return take(zz, chosen(zz, j), rows)

        for j in range(1, PLANE):
            e_out[zz * PLANE + j, rows] = taken(j)
            enc_copy(zz, j, r, parts).start()
        e_in[zz * PLANE, h, rows] = taken(0)
        half_copy(zz * PLANE, r, parts, h).start()

    def spread_in(p, r):
        zz, parts = plane_at(p), E_PARTS[p]
        for part in range(r * Z_PARTS // parts, (r + 1) * Z_PARTS // parts):
            set_copy(0, zz, part).wait_recv()
        spread(zz, r, parts)

    for kind in range(2):
        @pl.when(~is_end)
        def _():
            send_on(kind, z, own=True)
        x_copy(kind, z, own=True).start()
        y_copy(kind, z, own=True).start()
    for load in loads[:3]:
        load.wait()

    out_copy().start()
    blocks = [find(j) for j in range(PLANE)]
    last_blocks = [find_last(j) for j in range(PLANE)]

    def chosen(zz, j):
        return sum(jnp.where(zz == i, got, 0) for i, got in enumerate(blocks[j]))

    def plane_at(p):
        at_end = jnp.where(z == 0, p, NZ - 1 - p)
        between = jnp.where(p == 0, z, jnp.where(p == 1, mid, jnp.where(p == 2, near, far)))
        return jnp.where(is_end, at_end, between)

    def far_in(parts):
        for r in parts:
            set_copy(0, far, r).wait_recv()

    @pl.when(is_end)
    def _():
        one, two, three = plane_at(1), plane_at(2), plane_at(3)
        turn_k(z)
        turn_v(z)
        for r in range(E_PARTS[0]):
            spread(z, r, E_PARTS[0])
        pl.semaphore_wait(z_ready, 1)
        for kind in range(2):
            send_on(kind, z, own=True)
        send_set(z, range(Z_PARTS))
        across(0, 0).start()
        across(1, 1).start()
        rest_in(z)
        across(1, 0).start()
        across(0, 1).start()
        for kind in range(2):
            across(kind, 2).start()
        weights_in(0, one)
        weights_in(1, one)
        weights_in(0, two)
        turn_k(one)
        weights_in(1, two)
        turn_v(one)
        weights_in(0, three)
        turn_k(two)
        weights_in(1, three)
        turn_v(two)
        turn_k(three)
        spread_in(1, 0)
        turn_v(three)
        spread_in(1, 1)
        for k in (one, two, three):
            rest_in(k)

    @pl.when(~is_end)
    def _():
        turn_k(z)
        weights_in(0, mid)
        turn_v(z)
        weights_in(0, near, share=False)
        weights_in(1, mid)
        weights_in(1, near, share=False)
        send_set(z, [0])
        weights_in(0, far)
        turn_k(mid)
        weights_in(1, far)
        send_set(z, range(1, Z_PARTS))
        spread(z, 0, 2)
        turn_v(mid)
        spread(z, 1, 2)
        set_in(near, [0, 1])
        turn_k(far)
        set_in(mid, [0, 1])
        set_in(near, [2])
        turn_v(far)
        set_in(mid, [2, 3])
        set_in(near, [3])
        for r in range(2):
            far_in([2 * r, 2 * r + 1])
            pass_last(r)
            spread(mid, r, 2)
        for zz in (near, far):
            for r in range(2):
                spread(zz, r, 2)

    def weights_complete():
        for zz in (z, mid, far):
            rest_in(zz)
        for kind in range(2):
            for c in range(2):
                if (kind, c) in ((0, 0), (1, 1)):
                    arrive(kind, near * PLANE + columns[c])
        rest_in(near)

    def weights_sent():
        for zz in range(NZ):
            for kind in range(2):
                onward(zz, lambda: up_copy(kind, zz).wait_send(), lambda: down_copy(kind, zz).wait_send())

            @pl.when(is_end | (near != zz))
            def _():
                for kind in range(2):
                    x_copy(kind, zz).wait_send()
                    y_copy(kind, zz).wait_send()
                diag_k(zz).wait_send()
                diag_v(zz).wait_send()

        @pl.when(is_end)
        def _():
            for kind in range(2):
                for c in range(PLANE - 1):
                    across(kind, c).wait_send()

    def pass_halves(p, r):
        zz = plane_at(p)

        def one(j):
            enc_copy(zz, j, r, E_PARTS[p]).wait_recv()
            half_copy(zz * PLANE + j, r, E_PARTS[p], h).start()

        if p == NZ - 1:
            @pl.when(is_end)
            def _():
                one(0)
        for j in range(1, PLANE):
            one(j)

    def halves_in(p, r):
        for j in range(PLANE):
            half_copy(plane_at(p) * PLANE + j, r, E_PARTS[p], 1 - h).wait_recv()

    def project(zz, kind, first, count):
        slab = pl.ds(zz * PLANE, PLANE)
        rows = pl.ds(first, count)
        enc = e_in[slab, :, rows].reshape(PLANE * 2 * count, de)
        got = jnp.dot(enc, w[kind].reshape(de, width), preferred_element_type=jnp.float32)
        kv[kind, slab, :, rows] = got.astype(jnp.bfloat16).reshape(PLANE, 2, count, width)

    loads[3].wait()

    def taken_in(p, parts=None):
        parts = range(E_PARTS[p]) if parts is None else parts
        for r in parts:
            pass_halves(p, r)
        for r in parts:
            halves_in(p, r)

    def before(step):
        end_pieces = {0: [(2, 0)], 2: [(2, 1)]}

        @pl.when(is_end)
        def _():
            for p, r in end_pieces.get(step, []):
                spread_in(p, r)

        @pl.when(~is_end)
        def _():
            if step == 0:
                weights_complete()
                forward_last(0)
            if step == 2:
                forward_last(1)

        if step in (0, 2, 4):
            taken_in(step // 2)
        if step == 3:
            weights_sent()

    @pl.loop(0, 2 * (NZ - 1))
    def _(step):
        for k in range(2 * (NZ - 1)):
            @pl.when(step == k)
            def _():
                before(k)
        project(plane_at(step // 2), step % 2, 0, half)

    @pl.loop(0, 2)
    def _(side):
        for k in range(2):
            @pl.when(side == k)
            def _():
                taken_in(NZ - 1, range(k * E_PARTS[-1] // 2, (k + 1) * E_PARTS[-1] // 2))

        @pl.loop(0, 2)
        def _(kind):
            project(plane_at(NZ - 1), kind, pl.multiple_of(side * (half // 2), half // 2), half // 2)

    scale = HD ** -0.5

    def attend(c, full):
        one, two = slot_of(KNB * c), slot_of(KNB * c + 1)
        last = lax.broadcasted_iota(jnp.int32, (EDGE, HD), 0) == EDGE - 1
        edge = pl.ds(pl.multiple_of(c * CH + CH - EDGE, EDGE), EDGE)
        batch = 8

        def held(kind, cols):
            return jnp.concatenate(
                [kv[kind, one, :, :, cols].reshape(2 * half, HD),
                 kv[kind, two, :, :, cols].reshape(2 * half, HD)], axis=0)

        for first in range(0, width // HD, batch):
            spans = [slice(i * HD, (i + 1) * HD) for i in range(first, first + batch)]
            scores = []
            for cols in spans:
                q = q_pad[c, CH - EDGE:, cols]
                if full:
                    q = jnp.concatenate([q, q_pad[c + 1, :, cols]], axis=0)
                scores.append(
                    lax.dot_general(q, held(0, cols), NT, preferred_element_type=jnp.float32) * scale)
            tops = [jnp.max(score, axis=1, keepdims=True) for score in scores]
            expos = [jnp.exp(score - top) for score, top in zip(scores, tops)]
            sums = [jnp.sum(expo, axis=1, keepdims=True) for expo in expos]
            weights = [(expo / total).astype(jnp.bfloat16) for expo, total in zip(expos, sums)]
            outs = [
                jnp.dot(weight, held(1, cols), preferred_element_type=jnp.float32)
                for cols, weight in zip(spans, weights)]
            for cols, got in zip(spans, outs):
                old = att[0, edge, cols].astype(jnp.float32)
                att[0, edge, cols] = jnp.where(last, got[:EDGE], old).astype(jnp.bfloat16)
                if full:
                    att[0, pl.ds(pl.multiple_of(c * CH + CH, CH), CH), cols] = (
                        got[EDGE:].astype(jnp.bfloat16))

    att[0, 0:CH] = jnp.zeros((CH, width), jnp.bfloat16)

    @pl.loop(0, groups - 1)
    def _(c):
        attend(c, True)
        swap(c).start()

    attend(groups - 1, False)
    swap(groups - 1).start()

    def mix(t, side, held):
        rows = pl.ds(pl.multiple_of(t * OUT_TILE, OUT_TILE), OUT_TILE)
        return lax.dot_general(att[side], held[rows], NT, preferred_element_type=jnp.float32)

    loads[4].wait()
    mine = mix(0, 0, ow_own)
    out_copy().wait()
    for c in range(groups):
        swap(c).wait_recv()
    out_ref[:, 0:OUT_TILE] = (mine + mix(0, 1, ow_other)).astype(jnp.bfloat16)

    @pl.loop(1, feats // OUT_TILE)
    def _(t):
        got = mix(t, 0, ow_own) + mix(t, 1, ow_other)
        out_ref[:, pl.ds(pl.multiple_of(t * OUT_TILE, OUT_TILE), OUT_TILE)] = got.astype(jnp.bfloat16)

    for zz in range(NZ):
        for r in range(Z_PARTS):
            @pl.when(is_end | (zz != far))
            def _():
                onward(zz, lambda: set_copy(0, zz, r).wait_send(), lambda: set_copy(1, zz, r).wait_send())
    for p in range(NZ):
        zz = plane_at(p)
        for j in range(PLANE):
            for r in range(E_PARTS[p]):
                if j:
                    @pl.when(~is_end | (p < NZ - 1))
                    def _():
                        enc_copy(zz, j, r, E_PARTS[p]).wait_send()
                half_copy(zz * PLANE + j, r, E_PARTS[p], h).wait_send()

    @pl.when(~is_end)
    def _():
        for j in range(PLANE):
            for r in range(E_PARTS[-1]):
                if j:
                    pass_copy(j, r, E_PARTS[-1]).wait_send()
                last_copy(j, r, E_PARTS[-1]).wait_send()

    for c in range(groups):
        swap(c).wait_send()


def local_small(queries, key_weight, value_weight, out_weight, database, neighbours, placement):
    n = NZ * PLANE
    tok, width = queries.shape
    blk, half, de = database.shape
    feats = out_weight.shape[0] // 2
    groups = tok // CH
    sm = pl.BlockSpec(memory_space=pltpu.SMEM)
    hbm = pl.BlockSpec(memory_space=pl.ANY)
    dma = pltpu.SemaphoreType.DMA
    bf16 = jnp.bfloat16
    return pl.pallas_call(
        fused_kernel,
        out_shape=pltpu.VMEM((tok, feats), bf16),
        in_specs=[sm, sm] + [hbm] * 5,
        out_specs=pl.BlockSpec(memory_space=pltpu.VMEM),
        scratch_shapes=[
            pltpu.VMEM((2, n) + key_weight.shape, bf16),
            pltpu.VMEM((NZ,) + database.shape, bf16),
            pltpu.VMEM((n, half, de), bf16),
            pltpu.VMEM((n, 2, half, de), bf16),
            pltpu.VMEM((PLANE, half, de), bf16),
            pltpu.VMEM((PLANE, half, de), bf16),
            pltpu.VMEM((2, n, 2, half, width), bf16),
            pltpu.VMEM((groups, CH, width), bf16),
            pltpu.VMEM((2, tok, width), bf16),
            pltpu.VMEM((feats, width), bf16),
            pltpu.VMEM((feats, width), bf16),
            dma((2, NZ, Z_PARTS)), dma((NZ, Z_PARTS)), dma((n, max(E_PARTS))), dma((n, max(E_PARTS))),
            dma((n, max(E_PARTS))), dma((n, max(E_PARTS))), dma((2, 2, NZ)), dma((2, 2, NZ)), dma((2, NZ)),
            dma((2, PLANE - 1)), dma((2, n)), dma((2,)),
            *[dma((PLANE, max(E_PARTS)))] * 3, dma((groups,)), dma((groups,)), dma((5,)),
            pltpu.SemaphoreType.REGULAR,
        ],
        compiler_params=pltpu.CompilerParams(
            collective_id=0, has_side_effects=True, vmem_limit_bytes=VMEM_LIMIT),
    )(neighbours.T, placement, queries.reshape(groups, CH, width), key_weight, value_weight, out_weight, database)


def local_general(queries, key_weight, value_weight, out_weight, database, neighbours, placement):
    shard_count = lax.axis_size("shard")
    shard_self = lax.axis_index("shard")
    tok_rows = queries.shape[0]
    hd_local = queries.shape[1]
    heads_local = hd_local // HD
    per_dev = tok_rows // CH
    blk_local = database.shape[0]
    slots = placement[neighbours]
    needed = slots.reshape(shard_count, per_dev * KNB)
    owners = needed // blk_local
    matches = owners == shard_self
    hits = jnp.any(matches, axis=1)
    which = jnp.sum(jnp.where(matches, needed % blk_local, 0), axis=1)
    outgoing = jnp.zeros((shard_count,) + database.shape[1:], jnp.bfloat16)
    for b in range(blk_local):
        taken = (hits & (which == b))[:, None, None]
        outgoing = jnp.where(taken, database[b][None], outgoing)
    arrived = lax.all_to_all(outgoing, "shard", split_axis=0, concat_axis=0, tiled=True)
    own_need = lax.dynamic_slice_in_dim(needed, shard_self, 1, 0)[0]
    half_rows = jnp.concatenate(
        [
            lax.dynamic_slice_in_dim(arrived, own_need[i] // blk_local, 1, 0)
            for i in range(per_dev * KNB)
        ],
        axis=0,
    )
    encoded = lax.all_gather(half_rows, "head", axis=1, tiled=True)
    key_rows, val_rows = (
        lax.all_gather(key_weight, "shard", axis=0, tiled=True),
        lax.all_gather(value_weight, "shard", axis=0, tiled=True),
    )
    key_block = jnp.einsum(
        "brd,de->bre", encoded, key_rows, preferred_element_type=jnp.float32
    ).astype(jnp.bfloat16)
    val_block = jnp.einsum(
        "brd,de->bre", encoded, val_rows, preferred_element_type=jnp.float32
    ).astype(jnp.bfloat16)
    neighbour_len = encoded.shape[1]
    key_heads = key_block.reshape(per_dev, KNB * neighbour_len, heads_local, HD)
    val_heads = val_block.reshape(per_dev, KNB * neighbour_len, heads_local, HD)
    query_pad = jnp.concatenate(
        [queries[CH - 1 :], jnp.zeros((CH - 1, hd_local), jnp.bfloat16)], axis=0
    )
    query_pad = query_pad.reshape(per_dev, CH, heads_local, HD)
    score_scale = HD ** (-0.5)
    scores = (
        jnp.einsum("swhd,skhd->shwk", query_pad, key_heads, preferred_element_type=jnp.float32)
        * score_scale
    )
    row_max = jnp.max(scores, axis=-1, keepdims=True)
    expo = jnp.exp(scores - row_max)
    probs = expo / jnp.sum(expo, axis=-1, keepdims=True)
    weights_bf = probs.astype(jnp.bfloat16)
    window_out = jnp.einsum(
        "shwk,skhd->swhd", weights_bf, val_heads, preferred_element_type=jnp.float32
    )
    window_rows = window_out.astype(jnp.bfloat16).reshape(tok_rows, hd_local)
    attention = jnp.concatenate(
        [jnp.zeros((CH - 1, hd_local), jnp.bfloat16), window_rows[: tok_rows - (CH - 1)]], axis=0
    )
    partial_value = lax.dot_general(
        attention, out_weight, (((1,), (1,)), ((), ())), preferred_element_type=jnp.float32
    )
    return lax.psum_scatter(partial_value, "head", scatter_dimension=1, tiled=True).astype(
        jnp.bfloat16
    )


def solution(mesh):
    sizes = dict(mesh.shape)
    small = sizes["shard"] == NZ * PLANE and sizes["head"] == 2
    return jax.shard_map(
        local_small if small else local_general,
        mesh=mesh,
        in_specs=(
            P("shard", "head"),
            P("shard", "head"),
            P("shard", "head"),
            P(None, "head"),
            P("shard", "head", None),
            P(),
            P(),
        ),
        out_specs=P("shard", "head"),
        check_vma=False,
    )
```

```python
import jax
import jax.numpy as jnp
from jax import lax
from jax.experimental import pallas as pl
from jax.experimental.pallas import tpu as pltpu
from jax.sharding import PartitionSpec as P

HD = 128
CH = 64
KNB = 2
NZ, NY, NX = 4, 2, 2
PLANE = NY * NX
EDGE = 16
Z_PARTS = 4
E_PARTS = (2, 2, 2, 2)
OUT_TILE = 1024
MESH = pl.DeviceIdType.MESH
VMEM_LIMIT = 60 * 1024 * 1024
LOG2E = 1.4426950408889634
NT = (((1,), (1,)), ((), ()))


def shifted(shard, dy, dx):
    z, y, x = shard // PLANE, (shard // NX) % NY, shard % NX
    return z * PLANE + ((y + dy) % NY) * NX + (x + dx) % NX


def fused_kernel(
    near_hbm, place_hbm, q_ref, kw_ref, vw_ref, ow_ref, db_ref,
    out_ref,
    near_ref, place_ref, w, sets, e_out, e_in, pass_out, pass_in, kv, q_pad, att, ow_own, ow_other,
    s_send, s_recv, a_send, a_recv, f_send, f_recv, z_send, p_send, g_send, c_send, w_recv, o_sem,
    b_send, b_recv, n_send, t_send, t_recv, l_sem, z_ready,
):
    s = lax.axis_index("shard")
    h = lax.axis_index("head")
    z, y, x = s // PLANE, (s // NX) % NY, s % NX
    near_x = s + 1 - 2 * x
    near_y = s + NX * (1 - 2 * y)
    n = NZ * PLANE
    groups, _, width = q_ref.shape
    blk, half, de = db_ref.shape
    feats = ow_own.shape[0]
    picks = near_ref.shape[0] * near_ref.shape[1] // n
    is_end = (z == 0) | (z == NZ - 1)
    near, mid, far = jnp.where(z == 1, 0, NZ - 1), NZ - 1 - z, jnp.where(z == 1, NZ - 1, 0)

    barrier = pltpu.get_barrier_semaphore()

    def greet(to, head):
        pl.semaphore_signal(barrier, inc=1, device_id=(to, head), device_id_type=MESH)

    for j in range(1, PLANE):
        greet(shifted(s, j // NX, j % NX), h)
    greet(s, 1 - h)

    @pl.when((z == 0) | (z == 1))
    def _():
        greet(s + PLANE, h)

    @pl.when((z == 2) | (z == 3))
    def _():
        greet(s - PLANE, h)

    loads = [
        pltpu.make_async_copy(kw_ref, w.at[0, s], l_sem.at[0]),
        pltpu.make_async_copy(vw_ref, w.at[1, s], l_sem.at[1]),
        pltpu.make_async_copy(db_ref, sets.at[z], l_sem.at[2]),
        pltpu.make_async_copy(q_ref, q_pad, l_sem.at[3]),
        pltpu.make_async_copy(ow_ref.at[pl.ds(h * feats, feats)], ow_own, l_sem.at[4]),
    ]
    tables = [
        pltpu.make_async_copy(near_hbm, near_ref, l_sem.at[5]),
        pltpu.make_async_copy(place_hbm, place_ref, l_sem.at[6]),
    ]
    for load in loads + tables:
        load.start()

    @pl.when(is_end)
    def _():
        pl.semaphore_wait(barrier, PLANE)

    @pl.when(~is_end)
    def _():
        pl.semaphore_wait(barrier, PLANE + 2)

    @pl.when(z == 1)
    def _():
        pl.semaphore_signal(z_ready, inc=1, device_id=(s - PLANE, h), device_id_type=MESH)

    @pl.when(z == 2)
    def _():
        pl.semaphore_signal(z_ready, inc=1, device_id=(s + PLANE, h), device_id_type=MESH)

    def weight_copy(kind, chunk, to, sem, own=False):
        return pltpu.make_async_remote_copy(
            src_ref=(kw_ref, vw_ref)[kind] if own else w.at[kind, chunk], dst_ref=w.at[kind, chunk],
            send_sem=sem, recv_sem=w_recv.at[kind, chunk], device_id=(to, h), device_id_type=MESH)

    def column(zz):
        return zz * PLANE + y * NX + x

    def up_copy(kind, zz, own=False):
        return weight_copy(kind, column(zz), s + PLANE, z_send.at[0, kind, zz], own)

    def down_copy(kind, zz, own=False):
        return weight_copy(kind, column(zz), s - PLANE, z_send.at[1, kind, zz], own)

    def x_copy(kind, zz, own=False):
        return weight_copy(kind, column(zz), near_x, p_send.at[0, kind, zz], own)

    def y_copy(kind, zz, own=False):
        return weight_copy(kind, column(zz), near_y, p_send.at[1, kind, zz], own)

    def diag_k(zz):
        return weight_copy(0, zz * PLANE + y * NX + 1 - x, near_y, g_send.at[0, zz])

    def diag_v(zz):
        return weight_copy(1, zz * PLANE + (1 - y) * NX + x, near_x, g_send.at[1, zz])

    columns = (y * NX + 1 - x, (1 - y) * NX + x, (1 - y) * NX + 1 - x)

    def across(kind, c):
        to = jnp.where(z == 0, s + PLANE, s - PLANE)
        return weight_copy(kind, z * PLANE + columns[c], to, c_send.at[kind, c])

    def arrive(kind, chunk):
        weight_copy(kind, chunk, near_x, z_send.at[0, 0, 0]).wait_recv()

    z_rows = half // Z_PARTS

    def set_copy(way, zz, r):
        part = sets.at[zz, :, pl.ds(r * z_rows, z_rows)]
        return pltpu.make_async_remote_copy(
            src_ref=part, dst_ref=part, send_sem=s_send.at[way, zz, r], recv_sem=s_recv.at[zz, r],
            device_id=(s + PLANE - 2 * PLANE * way, h), device_id_type=MESH)

    def enc_copy(zz, j, r, parts):
        d = zz * PLANE + j
        rows = pl.ds(r * (half // parts), half // parts)
        return pltpu.make_async_remote_copy(
            src_ref=e_out.at[d, rows], dst_ref=e_in.at[d, h, rows], send_sem=a_send.at[d, r],
            recv_sem=a_recv.at[d, r], device_id=(shifted(s, j // NX, j % NX), h),
            device_id_type=MESH)

    def half_copy(d, r, parts, head):
        piece = e_in.at[d, head, pl.ds(r * (half // parts), half // parts)]
        return pltpu.make_async_remote_copy(
            src_ref=piece, dst_ref=piece, send_sem=f_send.at[d, r], recv_sem=f_recv.at[d, r],
            device_id=(s, 1 - h), device_id_type=MESH)

    def pass_copy(j, r, parts):
        rows = pl.ds(r * (half // parts), half // parts)
        return pltpu.make_async_remote_copy(
            src_ref=pass_out.at[j, rows], dst_ref=pass_in.at[j, rows], send_sem=b_send.at[j, r],
            recv_sem=b_recv.at[j, r], device_id=(shifted(s, j // NX, j % NX), h),
            device_id_type=MESH)

    def last_copy(j, r, parts):
        rows = pl.ds(r * (half // parts), half // parts)
        d = far * PLANE + j
        return pltpu.make_async_remote_copy(
            src_ref=(pass_in if j else pass_out).at[j, rows], dst_ref=e_in.at[d, h, rows],
            send_sem=n_send.at[j, r], recv_sem=a_recv.at[d, r],
            device_id=(jnp.where(z == 1, s - PLANE, s + PLANE), h), device_id_type=MESH)

    def out_copy():
        return pltpu.make_async_remote_copy(
            src_ref=ow_ref.at[pl.ds((1 - h) * feats, feats)], dst_ref=ow_other,
            send_sem=o_sem.at[0], recv_sem=o_sem.at[1], device_id=(s, 1 - h),
            device_id_type=MESH)

    def swap(c):
        rows = pl.ds(c * CH, CH)
        return pltpu.make_async_remote_copy(
            src_ref=att.at[0, rows], dst_ref=att.at[1, rows], send_sem=t_send.at[c],
            recv_sem=t_recv.at[c], device_id=(s, 1 - h), device_id_type=MESH)

    def pick(to, i):
        return place_ref[near_ref[i % KNB, to * (picks // KNB) + i // KNB]]

    def find(j):
        to = shifted(s, j // NX, j % NX)
        found = [jnp.int32(0)] * NZ
        for i in range(picks):
            slot = pick(to, i)
            owner, block = slot // blk, slot % blk
            found = [
                got + jnp.where(owner == column(zz), block, 0) for zz, got in enumerate(found)]
        return found

    def find_last(j):
        to = near * PLANE + shifted(s, j // NX, j % NX) % PLANE
        found = jnp.int32(0)
        for i in range(picks):
            slot = pick(to, i)
            found += jnp.where(slot // blk == column(far), slot % blk, 0)
        return found

    def slot_of(i):
        own = pick(s, i) // blk
        return own // PLANE * PLANE + (y + own // NX) % NY * NX + (x + own) % NX

    def onward(zz, up, down):
        @pl.when((zz <= z) & (z < NZ - 1))
        def _():
            up()

        @pl.when((zz >= z) & (z > 0))
        def _():
            down()

    def send_on(kind, zz, own=False):
        onward(
            zz, lambda: up_copy(kind, zz, own).start(), lambda: down_copy(kind, zz, own).start())

    def send_set(zz, parts):
        for r in parts:
            onward(zz, lambda: set_copy(0, zz, r).start(), lambda: set_copy(1, zz, r).start())

    def weights_in(kind, zz, share=True):
        arrive(kind, column(zz))
        send_on(kind, zz)
        if share:
            x_copy(kind, zz).start()
            y_copy(kind, zz).start()

    def turn_k(zz):
        arrive(0, zz * PLANE + columns[0])
        diag_k(zz).start()

    def turn_v(zz):
        arrive(1, zz * PLANE + columns[1])
        diag_v(zz).start()

    def rest_in(zz):
        arrive(1, zz * PLANE + columns[0])
        arrive(0, zz * PLANE + columns[1])
        for kind in range(2):
            arrive(kind, zz * PLANE + columns[2])

    def set_in(zz, parts):
        for r in parts:
            set_copy(0, zz, r).wait_recv()
            send_set(zz, [r])

    def take(zz, block, rows):
        got = sets[zz, 0, rows]
        for b in range(1, blk):
            got = lax.select(block == b, sets[zz, b, rows], got)
        return got

    def pass_last(r):
        parts = E_PARTS[-1]
        rows = pl.ds(r * (half // parts), half // parts)
        for j in range(1, PLANE):
            pass_out[j, rows] = take(far, last_blocks[j], rows)
            pass_copy(j, r, parts).start()
        pass_out[0, rows] = take(far, last_blocks[0], rows)
        last_copy(0, r, parts).start()

    def forward_last(r):
        for j in range(1, PLANE):
            pass_copy(j, r, E_PARTS[-1]).wait_recv()
            last_copy(j, r, E_PARTS[-1]).start()

    def spread(zz, r, parts):
        rows = pl.ds(r * (half // parts), half // parts)

        def taken(j):
            return take(zz, chosen(zz, j), rows)

        for j in range(1, PLANE):
            e_out[zz * PLANE + j, rows] = taken(j)
            enc_copy(zz, j, r, parts).start()
        e_in[zz * PLANE, h, rows] = taken(0)
        half_copy(zz * PLANE, r, parts, h).start()

    def spread_in(p, r):
        zz, parts = plane_at(p), E_PARTS[p]
        for part in range(r * Z_PARTS // parts, (r + 1) * Z_PARTS // parts):
            set_copy(0, zz, part).wait_recv()
        spread(zz, r, parts)

    for kind in range(2):
        @pl.when(~is_end)
        def _():
            send_on(kind, z, own=True)
        x_copy(kind, z, own=True).start()
        y_copy(kind, z, own=True).start()
    for load in loads[:3]:
        load.wait()

    out_copy().start()
    for table in tables:
        table.wait()
    blocks = [find(j) for j in range(PLANE)]
    last_blocks = [find_last(j) for j in range(PLANE)]

    def chosen(zz, j):
        return sum(jnp.where(zz == i, got, 0) for i, got in enumerate(blocks[j]))

    def plane_at(p):
        at_end = jnp.where(z == 0, p, NZ - 1 - p)
        between = jnp.where(p == 0, z, jnp.where(p == 1, mid, jnp.where(p == 2, near, far)))
        return jnp.where(is_end, at_end, between)

    def far_in(parts):
        for r in parts:
            set_copy(0, far, r).wait_recv()

    @pl.when(is_end)
    def _():
        one, two, three = plane_at(1), plane_at(2), plane_at(3)
        turn_k(z)
        turn_v(z)
        for r in range(E_PARTS[0]):
            spread(z, r, E_PARTS[0])
        pl.semaphore_wait(z_ready, 1)
        for kind in range(2):
            send_on(kind, z, own=True)
        send_set(z, range(Z_PARTS))
        across(0, 0).start()
        across(1, 1).start()
        rest_in(z)
        across(1, 0).start()
        across(0, 1).start()
        for kind in range(2):
            across(kind, 2).start()
        weights_in(0, one)
        weights_in(1, one)
        weights_in(0, two)
        turn_k(one)
        weights_in(1, two)
        turn_v(one)
        weights_in(0, three)
        turn_k(two)
        weights_in(1, three)
        turn_v(two)
        turn_k(three)
        spread_in(1, 0)
        turn_v(three)
        spread_in(1, 1)
        for k in (one, two, three):
            rest_in(k)

    @pl.when(~is_end)
    def _():
        turn_k(z)
        weights_in(0, mid)
        turn_v(z)
        weights_in(0, near, share=False)
        weights_in(1, mid)
        weights_in(1, near, share=False)
        send_set(z, [0])
        weights_in(0, far)
        turn_k(mid)
        weights_in(1, far)
        send_set(z, range(1, Z_PARTS))
        spread(z, 0, 2)
        turn_v(mid)
        spread(z, 1, 2)
        set_in(near, [0, 1])
        turn_k(far)
        set_in(mid, [0, 1])
        set_in(near, [2])
        turn_v(far)
        set_in(mid, [2, 3])
        set_in(near, [3])
        for r in range(2):
            far_in([2 * r, 2 * r + 1])
            pass_last(r)
            spread(mid, r, 2)
        for zz in (near, far):
            for r in range(2):
                spread(zz, r, 2)

    def weights_complete():
        for zz in (z, mid, far):
            rest_in(zz)
        for kind in range(2):
            for c in range(2):
                if (kind, c) in ((0, 0), (1, 1)):
                    arrive(kind, near * PLANE + columns[c])
        rest_in(near)

    def weights_sent():
        for zz in range(NZ):
            for kind in range(2):
                onward(zz, lambda: up_copy(kind, zz).wait_send(), lambda: down_copy(kind, zz).wait_send())

            @pl.when(is_end | (near != zz))
            def _():
                for kind in range(2):
                    x_copy(kind, zz).wait_send()
                    y_copy(kind, zz).wait_send()
                diag_k(zz).wait_send()
                diag_v(zz).wait_send()

        @pl.when(is_end)
        def _():
            for kind in range(2):
                for c in range(PLANE - 1):
                    across(kind, c).wait_send()

    def pass_halves(p, r):
        zz = plane_at(p)

        def one(j):
            enc_copy(zz, j, r, E_PARTS[p]).wait_recv()
            half_copy(zz * PLANE + j, r, E_PARTS[p], h).start()

        if p == NZ - 1:
            @pl.when(is_end)
            def _():
                one(0)
        for j in range(1, PLANE):
            one(j)

    def halves_in(p, r):
        for j in range(PLANE):
            half_copy(plane_at(p) * PLANE + j, r, E_PARTS[p], 1 - h).wait_recv()

    def project(zz, kind, first, count):
        slab = pl.ds(zz * PLANE, PLANE)
        rows = pl.ds(first, count)
        enc = e_in[slab, :, rows].reshape(PLANE * 2 * count, de)
        got = jnp.dot(enc, w[kind].reshape(de, width), preferred_element_type=jnp.float32)
        kv[kind, slab, :, rows] = got.astype(jnp.bfloat16).reshape(PLANE, 2, count, width)

    loads[3].wait()

    def taken_in(p, parts=None):
        parts = range(E_PARTS[p]) if parts is None else parts
        for r in parts:
            pass_halves(p, r)
        for r in parts:
            halves_in(p, r)

    def before(step):
        end_pieces = {0: [(2, 0)], 1: [(2, 1)]}

        @pl.when(is_end)
        def _():
            for p, r in end_pieces.get(step, []):
                spread_in(p, r)

        @pl.when(~is_end)
        def _():
            if step == 0:
                weights_complete()
                forward_last(0)
            if step == 1:
                forward_last(1)

        taken_in(step)
        if step == 1:
            weights_sent()

    @pl.loop(0, NZ - 1)
    def _(p):
        for k in range(NZ - 1):
            @pl.when(p == k)
            def _():
                before(k)
        for kind in range(2):
            project(plane_at(p), kind, 0, half)

    taken_in(NZ - 1)
    for kind in range(2):
        project(plane_at(NZ - 1), kind, 0, half)

    scale = HD ** -0.5 * LOG2E

    def attend(c, full):
        one, two = slot_of(KNB * c), slot_of(KNB * c + 1)
        last = lax.broadcasted_iota(jnp.int32, (EDGE, HD), 0) == EDGE - 1
        edge = pl.ds(pl.multiple_of(c * CH + CH - EDGE, EDGE), EDGE)
        batch = 8

        def held(kind, cols):
            return jnp.concatenate(
                [kv[kind, one, :, :, cols].reshape(2 * half, HD),
                 kv[kind, two, :, :, cols].reshape(2 * half, HD)], axis=0)

        for first in range(0, width // HD, batch):
            spans = [slice(i * HD, (i + 1) * HD) for i in range(first, first + batch)]
            scores = []
            for cols in spans:
                q = q_pad[c, CH - EDGE:, cols]
                if full:
                    q = jnp.concatenate([q, q_pad[c + 1, :, cols]], axis=0)
                scores.append(
                    lax.dot_general(q, held(0, cols), NT, preferred_element_type=jnp.float32))
            tops = [jnp.max(score, axis=1, keepdims=True) for score in scores]
            expos = [jnp.exp2((score - top) * scale) for score, top in zip(scores, tops)]
            sums = [jnp.sum(expo, axis=1, keepdims=True) for expo in expos]
            weights = [(expo * (1.0 / total)).astype(jnp.bfloat16) for expo, total in zip(expos, sums)]
            outs = [
                jnp.dot(weight, held(1, cols), preferred_element_type=jnp.float32)
                for cols, weight in zip(spans, weights)]
            for cols, got in zip(spans, outs):
                old = att[0, edge, cols].astype(jnp.float32)
                att[0, edge, cols] = jnp.where(last, got[:EDGE], old).astype(jnp.bfloat16)
                if full:
                    att[0, pl.ds(pl.multiple_of(c * CH + CH, CH), CH), cols] = (
                        got[EDGE:].astype(jnp.bfloat16))

    att[0, 0:CH] = jnp.zeros((CH, width), jnp.bfloat16)

    for c in range(groups - 1):
        attend(c, True)
        swap(c).start()

    attend(groups - 1, False)
    swap(groups - 1).start()

    def mix(t, side, held):
        rows = pl.ds(pl.multiple_of(t * OUT_TILE, OUT_TILE), OUT_TILE)
        return lax.dot_general(att[side], held[rows], NT, preferred_element_type=jnp.float32)

    loads[4].wait()
    mine = mix(0, 0, ow_own)
    out_copy().wait()
    for c in range(groups):
        swap(c).wait_recv()
    out_ref[:, 0:OUT_TILE] = (mine + mix(0, 1, ow_other)).astype(jnp.bfloat16)

    @pl.loop(1, feats // OUT_TILE)
    def _(t):
        got = mix(t, 0, ow_own) + mix(t, 1, ow_other)
        out_ref[:, pl.ds(pl.multiple_of(t * OUT_TILE, OUT_TILE), OUT_TILE)] = got.astype(jnp.bfloat16)

    for zz in range(NZ):
        for r in range(Z_PARTS):
            @pl.when(is_end | (zz != far))
            def _():
                onward(zz, lambda: set_copy(0, zz, r).wait_send(), lambda: set_copy(1, zz, r).wait_send())
    for p in range(NZ):
        zz = plane_at(p)
        for j in range(PLANE):
            for r in range(E_PARTS[p]):
                if j:
                    @pl.when(~is_end | (p < NZ - 1))
                    def _():
                        enc_copy(zz, j, r, E_PARTS[p]).wait_send()
                half_copy(zz * PLANE + j, r, E_PARTS[p], h).wait_send()

    @pl.when(~is_end)
    def _():
        for j in range(PLANE):
            for r in range(E_PARTS[-1]):
                if j:
                    pass_copy(j, r, E_PARTS[-1]).wait_send()
                last_copy(j, r, E_PARTS[-1]).wait_send()

    for c in range(groups):
        swap(c).wait_send()


def local_small(queries, key_weight, value_weight, out_weight, database, neighbours, placement):
    n = NZ * PLANE
    tok, width = queries.shape
    blk, half, de = database.shape
    feats = out_weight.shape[0] // 2
    groups = tok // CH
    hbm = pl.BlockSpec(memory_space=pl.ANY)
    dma = pltpu.SemaphoreType.DMA
    bf16 = jnp.bfloat16
    return pl.pallas_call(
        fused_kernel,
        out_shape=pltpu.VMEM((tok, feats), bf16),
        in_specs=[hbm] * 7,
        out_specs=pl.BlockSpec(memory_space=pltpu.VMEM),
        scratch_shapes=[
            pltpu.SMEM((KNB, neighbours.shape[0]), jnp.int32),
            pltpu.SMEM(placement.shape, jnp.int32),
            pltpu.VMEM((2, n) + key_weight.shape, bf16),
            pltpu.VMEM((NZ,) + database.shape, bf16),
            pltpu.VMEM((n, half, de), bf16),
            pltpu.VMEM((n, 2, half, de), bf16),
            pltpu.VMEM((PLANE, half, de), bf16),
            pltpu.VMEM((PLANE, half, de), bf16),
            pltpu.VMEM((2, n, 2, half, width), bf16),
            pltpu.VMEM((groups, CH, width), bf16),
            pltpu.VMEM((2, tok, width), bf16),
            pltpu.VMEM((feats, width), bf16),
            pltpu.VMEM((feats, width), bf16),
            dma((2, NZ, Z_PARTS)), dma((NZ, Z_PARTS)), dma((n, max(E_PARTS))), dma((n, max(E_PARTS))),
            dma((n, max(E_PARTS))), dma((n, max(E_PARTS))), dma((2, 2, NZ)), dma((2, 2, NZ)), dma((2, NZ)),
            dma((2, PLANE - 1)), dma((2, n)), dma((2,)),
            *[dma((PLANE, max(E_PARTS)))] * 3, dma((groups,)), dma((groups,)), dma((7,)),
            pltpu.SemaphoreType.REGULAR,
        ],
        compiler_params=pltpu.CompilerParams(
            collective_id=0, has_side_effects=True, vmem_limit_bytes=VMEM_LIMIT),
    )(neighbours.T, placement, queries.reshape(groups, CH, width), key_weight, value_weight, out_weight, database)


def local_general(queries, key_weight, value_weight, out_weight, database, neighbours, placement):
    shard_count = lax.axis_size("shard")
    shard_self = lax.axis_index("shard")
    tok_rows = queries.shape[0]
    hd_local = queries.shape[1]
    heads_local = hd_local // HD
    per_dev = tok_rows // CH
    blk_local = database.shape[0]
    slots = placement[neighbours]
    needed = slots.reshape(shard_count, per_dev * KNB)
    owners = needed // blk_local
    matches = owners == shard_self
    hits = jnp.any(matches, axis=1)
    which = jnp.sum(jnp.where(matches, needed % blk_local, 0), axis=1)
    outgoing = jnp.zeros((shard_count,) + database.shape[1:], jnp.bfloat16)
    for b in range(blk_local):
        taken = (hits & (which == b))[:, None, None]
        outgoing = jnp.where(taken, database[b][None], outgoing)
    arrived = lax.all_to_all(outgoing, "shard", split_axis=0, concat_axis=0, tiled=True)
    own_need = lax.dynamic_slice_in_dim(needed, shard_self, 1, 0)[0]
    half_rows = jnp.concatenate(
        [
            lax.dynamic_slice_in_dim(arrived, own_need[i] // blk_local, 1, 0)
            for i in range(per_dev * KNB)
        ],
        axis=0,
    )
    encoded = lax.all_gather(half_rows, "head", axis=1, tiled=True)
    key_rows, val_rows = (
        lax.all_gather(key_weight, "shard", axis=0, tiled=True),
        lax.all_gather(value_weight, "shard", axis=0, tiled=True),
    )
    key_block = jnp.einsum(
        "brd,de->bre", encoded, key_rows, preferred_element_type=jnp.float32
    ).astype(jnp.bfloat16)
    val_block = jnp.einsum(
        "brd,de->bre", encoded, val_rows, preferred_element_type=jnp.float32
    ).astype(jnp.bfloat16)
    neighbour_len = encoded.shape[1]
    key_heads = key_block.reshape(per_dev, KNB * neighbour_len, heads_local, HD)
    val_heads = val_block.reshape(per_dev, KNB * neighbour_len, heads_local, HD)
    query_pad = jnp.concatenate(
        [queries[CH - 1 :], jnp.zeros((CH - 1, hd_local), jnp.bfloat16)], axis=0
    )
    query_pad = query_pad.reshape(per_dev, CH, heads_local, HD)
    score_scale = HD ** (-0.5)
    scores = (
        jnp.einsum("swhd,skhd->shwk", query_pad, key_heads, preferred_element_type=jnp.float32)
        * score_scale
    )
    row_max = jnp.max(scores, axis=-1, keepdims=True)
    expo = jnp.exp(scores - row_max)
    probs = expo / jnp.sum(expo, axis=-1, keepdims=True)
    weights_bf = probs.astype(jnp.bfloat16)
    window_out = jnp.einsum(
        "shwk,skhd->swhd", weights_bf, val_heads, preferred_element_type=jnp.float32
    )
    window_rows = window_out.astype(jnp.bfloat16).reshape(tok_rows, hd_local)
    attention = jnp.concatenate(
        [jnp.zeros((CH - 1, hd_local), jnp.bfloat16), window_rows[: tok_rows - (CH - 1)]], axis=0
    )
    partial_value = lax.dot_general(
        attention, out_weight, (((1,), (1,)), ((), ())), preferred_element_type=jnp.float32
    )
    return lax.psum_scatter(partial_value, "head", scatter_dimension=1, tiled=True).astype(
        jnp.bfloat16
    )


def solution(mesh):
    sizes = dict(mesh.shape)
    small = sizes["shard"] == NZ * PLANE and sizes["head"] == 2
    return jax.shard_map(
        local_small if small else local_general,
        mesh=mesh,
        in_specs=(
            P("shard", "head"),
            P("shard", "head"),
            P("shard", "head"),
            P(None, "head"),
            P("shard", "head", None),
            P(),
            P(),
        ),
        out_specs=P("shard", "head"),
        check_vma=False,
    )
```

```python
import jax
import jax.numpy as jnp
from jax import lax
from jax.experimental import pallas as pl
from jax.experimental.pallas import tpu as pltpu
from jax.sharding import PartitionSpec as P

HD = 128
CH = 64
KNB = 2
NZ, NY, NX = 4, 2, 2
PLANE = NY * NX
EDGE = 16
Z_PARTS = 4
E_PARTS = (2, 2, 2, 2)
OUT_TILE = 1024
MESH = pl.DeviceIdType.MESH
VMEM_LIMIT = 60 * 1024 * 1024
LOG2E = 1.4426950408889634
NT = (((1,), (1,)), ((), ()))


def shifted(shard, dy, dx):
    z, y, x = shard // PLANE, (shard // NX) % NY, shard % NX
    return z * PLANE + ((y + dy) % NY) * NX + (x + dx) % NX


def fused_kernel(
    near_hbm, place_hbm, q_ref, kw_ref, vw_ref, ow_ref, db_ref,
    out_ref,
    near_ref, place_ref, w, sets, e_out, e_in, pass_out, pass_in, kv, q_pad, att, ow_own, ow_other,
    s_send, s_recv, a_send, a_recv, f_send, f_recv, z_send, p_send, g_send, c_send, w_recv, o_sem,
    b_send, b_recv, n_send, t_send, t_recv, l_sem, z_ready,
):
    s = lax.axis_index("shard")
    h = lax.axis_index("head")
    z, y, x = s // PLANE, (s // NX) % NY, s % NX
    near_x = s + 1 - 2 * x
    near_y = s + NX * (1 - 2 * y)
    n = NZ * PLANE
    groups, _, width = q_ref.shape
    blk, half, de = db_ref.shape
    feats = ow_own.shape[0]
    picks = near_ref.shape[0] * near_ref.shape[1] // n
    is_end = (z == 0) | (z == NZ - 1)
    near, mid, far = jnp.where(z == 1, 0, NZ - 1), NZ - 1 - z, jnp.where(z == 1, NZ - 1, 0)

    barrier = pltpu.get_barrier_semaphore()

    def greet(to, head):
        pl.semaphore_signal(barrier, inc=1, device_id=(to, head), device_id_type=MESH)

    for j in range(1, PLANE):
        greet(shifted(s, j // NX, j % NX), h)
    greet(s, 1 - h)

    @pl.when((z == 0) | (z == 1))
    def _():
        greet(s + PLANE, h)

    @pl.when((z == 2) | (z == 3))
    def _():
        greet(s - PLANE, h)

    loads = [
        pltpu.make_async_copy(kw_ref, w.at[0, s], l_sem.at[0]),
        pltpu.make_async_copy(vw_ref, w.at[1, s], l_sem.at[1]),
        pltpu.make_async_copy(db_ref, sets.at[z], l_sem.at[2]),
        pltpu.make_async_copy(q_ref, q_pad, l_sem.at[3]),
        pltpu.make_async_copy(ow_ref.at[pl.ds(h * feats, feats)], ow_own, l_sem.at[4]),
    ]
    tables = [
        pltpu.make_async_copy(near_hbm, near_ref, l_sem.at[5]),
        pltpu.make_async_copy(place_hbm, place_ref, l_sem.at[6]),
    ]
    for load in loads + tables:
        load.start()

    @pl.when(is_end)
    def _():
        pl.semaphore_wait(barrier, PLANE)

    @pl.when(~is_end)
    def _():
        pl.semaphore_wait(barrier, PLANE + 2)

    @pl.when(z == 1)
    def _():
        pl.semaphore_signal(z_ready, inc=1, device_id=(s - PLANE, h), device_id_type=MESH)

    @pl.when(z == 2)
    def _():
        pl.semaphore_signal(z_ready, inc=1, device_id=(s + PLANE, h), device_id_type=MESH)

    def weight_copy(kind, chunk, to, sem, own=False):
        return pltpu.make_async_remote_copy(
            src_ref=(kw_ref, vw_ref)[kind] if own else w.at[kind, chunk], dst_ref=w.at[kind, chunk],
            send_sem=sem, recv_sem=w_recv.at[kind, chunk], device_id=(to, h), device_id_type=MESH)

    def column(zz):
        return zz * PLANE + y * NX + x

    def up_copy(kind, zz, own=False):
        return weight_copy(kind, column(zz), s + PLANE, z_send.at[0, kind, zz], own)

    def down_copy(kind, zz, own=False):
        return weight_copy(kind, column(zz), s - PLANE, z_send.at[1, kind, zz], own)

    def x_copy(kind, zz, own=False):
        return weight_copy(kind, column(zz), near_x, p_send.at[0, kind, zz], own)

    def y_copy(kind, zz, own=False):
        return weight_copy(kind, column(zz), near_y, p_send.at[1, kind, zz], own)

    def diag_k(zz):
        return weight_copy(0, zz * PLANE + y * NX + 1 - x, near_y, g_send.at[0, zz])

    def diag_v(zz):
        return weight_copy(1, zz * PLANE + (1 - y) * NX + x, near_x, g_send.at[1, zz])

    columns = (y * NX + 1 - x, (1 - y) * NX + x, (1 - y) * NX + 1 - x)

    def across(kind, c):
        to = jnp.where(z == 0, s + PLANE, s - PLANE)
        return weight_copy(kind, z * PLANE + columns[c], to, c_send.at[kind, c])

    def arrive(kind, chunk):
        weight_copy(kind, chunk, near_x, z_send.at[0, 0, 0]).wait_recv()

    z_rows = half // Z_PARTS

    def set_copy(way, zz, r):
        part = sets.at[zz, :, pl.ds(r * z_rows, z_rows)]
        return pltpu.make_async_remote_copy(
            src_ref=part, dst_ref=part, send_sem=s_send.at[way, zz, r], recv_sem=s_recv.at[zz, r],
            device_id=(s + PLANE - 2 * PLANE * way, h), device_id_type=MESH)

    def enc_copy(zz, j, r, parts):
        d = zz * PLANE + j
        rows = pl.ds(r * (half // parts), half // parts)
        return pltpu.make_async_remote_copy(
            src_ref=e_out.at[d, rows], dst_ref=e_in.at[d, h, rows], send_sem=a_send.at[d, r],
            recv_sem=a_recv.at[d, r], device_id=(shifted(s, j // NX, j % NX), h),
            device_id_type=MESH)

    def half_copy(d, r, parts, head):
        piece = e_in.at[d, head, pl.ds(r * (half // parts), half // parts)]
        return pltpu.make_async_remote_copy(
            src_ref=piece, dst_ref=piece, send_sem=f_send.at[d, r], recv_sem=f_recv.at[d, r],
            device_id=(s, 1 - h), device_id_type=MESH)

    def pass_copy(j, r, parts):
        rows = pl.ds(r * (half // parts), half // parts)
        return pltpu.make_async_remote_copy(
            src_ref=pass_out.at[j, rows], dst_ref=pass_in.at[j, rows], send_sem=b_send.at[j, r],
            recv_sem=b_recv.at[j, r], device_id=(shifted(s, j // NX, j % NX), h),
            device_id_type=MESH)

    def last_copy(j, r, parts):
        rows = pl.ds(r * (half // parts), half // parts)
        d = far * PLANE + j
        return pltpu.make_async_remote_copy(
            src_ref=(pass_in if j else pass_out).at[j, rows], dst_ref=e_in.at[d, h, rows],
            send_sem=n_send.at[j, r], recv_sem=a_recv.at[d, r],
            device_id=(jnp.where(z == 1, s - PLANE, s + PLANE), h), device_id_type=MESH)

    def out_copy():
        return pltpu.make_async_remote_copy(
            src_ref=ow_ref.at[pl.ds((1 - h) * feats, feats)], dst_ref=ow_other,
            send_sem=o_sem.at[0], recv_sem=o_sem.at[1], device_id=(s, 1 - h),
            device_id_type=MESH)

    def swap(c):
        rows = pl.ds(c * CH, CH)
        return pltpu.make_async_remote_copy(
            src_ref=att.at[0, rows], dst_ref=att.at[1, rows], send_sem=t_send.at[c],
            recv_sem=t_recv.at[c], device_id=(s, 1 - h), device_id_type=MESH)

    def pick(to, i):
        return place_ref[near_ref[i % KNB, to * (picks // KNB) + i // KNB]]

    def find(j):
        to = shifted(s, j // NX, j % NX)
        found = [jnp.int32(0)] * NZ
        for i in range(picks):
            slot = pick(to, i)
            owner, block = slot // blk, slot % blk
            found = [
                got + jnp.where(owner == column(zz), block, 0) for zz, got in enumerate(found)]
        return found

    def find_last(j):
        to = near * PLANE + shifted(s, j // NX, j % NX) % PLANE
        found = jnp.int32(0)
        for i in range(picks):
            slot = pick(to, i)
            found += jnp.where(slot // blk == column(far), slot % blk, 0)
        return found

    def slot_of(i):
        own = pick(s, i) // blk
        return own // PLANE * PLANE + (y + own // NX) % NY * NX + (x + own) % NX

    def onward(zz, up, down):
        @pl.when((zz <= z) & (z < NZ - 1))
        def _():
            up()

        @pl.when((zz >= z) & (z > 0))
        def _():
            down()

    def send_on(kind, zz, own=False):
        onward(
            zz, lambda: up_copy(kind, zz, own).start(), lambda: down_copy(kind, zz, own).start())

    def send_set(zz, parts):
        for r in parts:
            onward(zz, lambda: set_copy(0, zz, r).start(), lambda: set_copy(1, zz, r).start())

    def weights_in(kind, zz, share=True):
        arrive(kind, column(zz))
        send_on(kind, zz)
        if share:
            x_copy(kind, zz).start()
            y_copy(kind, zz).start()

    def turn_k(zz):
        arrive(0, zz * PLANE + columns[0])
        diag_k(zz).start()

    def turn_v(zz):
        arrive(1, zz * PLANE + columns[1])
        diag_v(zz).start()

    def rest_in(zz):
        arrive(1, zz * PLANE + columns[0])
        arrive(0, zz * PLANE + columns[1])
        for kind in range(2):
            arrive(kind, zz * PLANE + columns[2])

    def set_in(zz, parts):
        for r in parts:
            set_copy(0, zz, r).wait_recv()
            send_set(zz, [r])

    def take(zz, block, rows):
        got = sets[zz, 0, rows]
        for b in range(1, blk):
            got = lax.select(block == b, sets[zz, b, rows], got)
        return got

    def pass_last(r):
        parts = E_PARTS[-1]
        rows = pl.ds(r * (half // parts), half // parts)
        for j in range(1, PLANE):
            pass_out[j, rows] = take(far, last_blocks[j], rows)
            pass_copy(j, r, parts).start()
        pass_out[0, rows] = take(far, last_blocks[0], rows)
        last_copy(0, r, parts).start()

    def forward_last(r):
        for j in range(1, PLANE):
            pass_copy(j, r, E_PARTS[-1]).wait_recv()
            last_copy(j, r, E_PARTS[-1]).start()

    def spread(zz, r, parts):
        rows = pl.ds(r * (half // parts), half // parts)

        def taken(j):
            return take(zz, chosen(zz, j), rows)

        for j in range(1, PLANE):
            e_out[zz * PLANE + j, rows] = taken(j)
            enc_copy(zz, j, r, parts).start()
        e_in[zz * PLANE, h, rows] = taken(0)
        half_copy(zz * PLANE, r, parts, h).start()

    def spread_in(p, r):
        zz, parts = plane_at(p), E_PARTS[p]
        for part in range(r * Z_PARTS // parts, (r + 1) * Z_PARTS // parts):
            set_copy(0, zz, part).wait_recv()
        spread(zz, r, parts)

    for kind in range(2):
        @pl.when(~is_end)
        def _():
            send_on(kind, z, own=True)
        x_copy(kind, z, own=True).start()
        y_copy(kind, z, own=True).start()
    for load in loads[:3]:
        load.wait()

    out_copy().start()
    for table in tables:
        table.wait()
    blocks = [find(j) for j in range(PLANE)]
    last_blocks = [find_last(j) for j in range(PLANE)]

    def chosen(zz, j):
        return sum(jnp.where(zz == i, got, 0) for i, got in enumerate(blocks[j]))

    def plane_at(p):
        at_end = jnp.where(z == 0, p, NZ - 1 - p)
        between = jnp.where(p == 0, z, jnp.where(p == 1, mid, jnp.where(p == 2, near, far)))
        return jnp.where(is_end, at_end, between)

    def far_in(parts):
        for r in parts:
            set_copy(0, far, r).wait_recv()

    @pl.when(is_end)
    def _():
        one, two, three = plane_at(1), plane_at(2), plane_at(3)
        turn_k(z)
        turn_v(z)
        for r in range(E_PARTS[0]):
            spread(z, r, E_PARTS[0])
        pl.semaphore_wait(z_ready, 1)
        for kind in range(2):
            send_on(kind, z, own=True)
        send_set(z, range(Z_PARTS))
        across(0, 0).start()
        across(1, 1).start()
        rest_in(z)
        across(1, 0).start()
        across(0, 1).start()
        for kind in range(2):
            across(kind, 2).start()
        weights_in(0, one)
        weights_in(1, one)
        weights_in(0, two)
        turn_k(one)
        weights_in(1, two)
        turn_v(one)
        weights_in(0, three)
        turn_k(two)
        weights_in(1, three)
        turn_v(two)
        turn_k(three)
        spread_in(1, 0)
        turn_v(three)
        spread_in(1, 1)
        for k in (one, two, three):
            rest_in(k)

    @pl.when(~is_end)
    def _():
        turn_k(z)
        weights_in(0, mid)
        turn_v(z)
        weights_in(0, near, share=False)
        weights_in(1, mid)
        weights_in(1, near, share=False)
        send_set(z, [0])
        weights_in(0, far)
        turn_k(mid)
        weights_in(1, far)
        send_set(z, range(1, Z_PARTS))
        spread(z, 0, 2)
        turn_v(mid)
        spread(z, 1, 2)
        set_in(near, [0, 1])
        turn_k(far)
        set_in(mid, [0, 1])
        set_in(near, [2])
        turn_v(far)
        set_in(mid, [2, 3])
        set_in(near, [3])
        for r in range(2):
            far_in([2 * r, 2 * r + 1])
            pass_last(r)
            spread(mid, r, 2)
        for zz in (near, far):
            for r in range(2):
                spread(zz, r, 2)

    def weights_complete():
        for zz in (z, mid, far):
            rest_in(zz)
        for kind in range(2):
            for c in range(2):
                if (kind, c) in ((0, 0), (1, 1)):
                    arrive(kind, near * PLANE + columns[c])
        rest_in(near)

    def weights_sent():
        for zz in range(NZ):
            for kind in range(2):
                onward(zz, lambda: up_copy(kind, zz).wait_send(), lambda: down_copy(kind, zz).wait_send())

            @pl.when(is_end | (near != zz))
            def _():
                for kind in range(2):
                    x_copy(kind, zz).wait_send()
                    y_copy(kind, zz).wait_send()
                diag_k(zz).wait_send()
                diag_v(zz).wait_send()

        @pl.when(is_end)
        def _():
            for kind in range(2):
                for c in range(PLANE - 1):
                    across(kind, c).wait_send()

    def pass_halves(p, r):
        zz = plane_at(p)

        def one(j):
            enc_copy(zz, j, r, E_PARTS[p]).wait_recv()
            half_copy(zz * PLANE + j, r, E_PARTS[p], h).start()

        if p == NZ - 1:
            @pl.when(is_end)
            def _():
                one(0)
        for j in range(1, PLANE):
            one(j)

    def halves_in(p, r):
        for j in range(PLANE):
            half_copy(plane_at(p) * PLANE + j, r, E_PARTS[p], 1 - h).wait_recv()

    def project(zz, kind, first, count):
        slab = pl.ds(zz * PLANE, PLANE)
        rows = pl.ds(first, count)
        enc = e_in[slab, :, rows].reshape(PLANE * 2 * count, de)
        got = jnp.dot(enc, w[kind].reshape(de, width), preferred_element_type=jnp.float32)
        kv[kind, slab, :, rows] = got.astype(jnp.bfloat16).reshape(PLANE, 2, count, width)

    loads[3].wait()

    def taken_in(p, parts=None):
        parts = range(E_PARTS[p]) if parts is None else parts
        for r in parts:
            pass_halves(p, r)
        for r in parts:
            halves_in(p, r)

    def before(step):
        end_pieces = {0: [(2, 0)], 1: [(2, 1)]}

        @pl.when(is_end)
        def _():
            for p, r in end_pieces.get(step, []):
                spread_in(p, r)

        @pl.when(~is_end)
        def _():
            if step == 0:
                weights_complete()
                forward_last(0)
            if step == 1:
                forward_last(1)

        taken_in(step)

    @pl.loop(0, NZ - 1)
    def _(p):
        for k in range(NZ - 1):
            @pl.when(p == k)
            def _():
                before(k)
        for kind in range(2):
            project(plane_at(p), kind, 0, half)

    taken_in(NZ - 1)
    for kind in range(2):
        project(plane_at(NZ - 1), kind, 0, half)

    scale = HD ** -0.5 * LOG2E

    def attend(c, full):
        one, two = slot_of(KNB * c), slot_of(KNB * c + 1)
        last = lax.broadcasted_iota(jnp.int32, (EDGE, HD), 0) == EDGE - 1
        edge = pl.ds(pl.multiple_of(c * CH + CH - EDGE, EDGE), EDGE)
        batch = 8

        def held(kind, cols):
            return jnp.concatenate(
                [kv[kind, one, :, :, cols].reshape(2 * half, HD),
                 kv[kind, two, :, :, cols].reshape(2 * half, HD)], axis=0)

        for first in range(0, width // HD, batch):
            spans = [slice(i * HD, (i + 1) * HD) for i in range(first, first + batch)]
            scores = []
            for cols in spans:
                q = q_pad[c, CH - EDGE:, cols]
                if full:
                    q = jnp.concatenate([q, q_pad[c + 1, :, cols]], axis=0)
                scores.append(
                    lax.dot_general(q, held(0, cols), NT, preferred_element_type=jnp.float32))
            tops = [jnp.max(score, axis=1, keepdims=True) for score in scores]
            expos = [jnp.exp2((score - top) * scale) for score, top in zip(scores, tops)]
            sums = [jnp.sum(expo, axis=1, keepdims=True) for expo in expos]
            weights = [(expo * (1.0 / total)).astype(jnp.bfloat16) for expo, total in zip(expos, sums)]
            outs = [
                jnp.dot(weight, held(1, cols), preferred_element_type=jnp.float32)
                for cols, weight in zip(spans, weights)]
            for cols, got in zip(spans, outs):
                old = att[0, edge, cols].astype(jnp.float32)
                att[0, edge, cols] = jnp.where(last, got[:EDGE], old).astype(jnp.bfloat16)
                if full:
                    att[0, pl.ds(pl.multiple_of(c * CH + CH, CH), CH), cols] = (
                        got[EDGE:].astype(jnp.bfloat16))

    att[0, 0:CH] = jnp.zeros((CH, width), jnp.bfloat16)

    for c in range(groups - 1):
        attend(c, True)
        swap(c).start()

    attend(groups - 1, False)
    swap(groups - 1).start()

    def mix(t, side, held):
        rows = pl.ds(pl.multiple_of(t * OUT_TILE, OUT_TILE), OUT_TILE)
        return lax.dot_general(att[side], held[rows], NT, preferred_element_type=jnp.float32)

    loads[4].wait()
    mine = mix(0, 0, ow_own)
    out_copy().wait()
    for c in range(groups):
        swap(c).wait_recv()
    out_ref[:, 0:OUT_TILE] = (mine + mix(0, 1, ow_other)).astype(jnp.bfloat16)

    for t in range(1, feats // OUT_TILE):
        got = mix(t, 0, ow_own) + mix(t, 1, ow_other)
        out_ref[:, pl.ds(pl.multiple_of(t * OUT_TILE, OUT_TILE), OUT_TILE)] = got.astype(jnp.bfloat16)

    weights_sent()
    for zz in range(NZ):
        for r in range(Z_PARTS):
            @pl.when(is_end | (zz != far))
            def _():
                onward(zz, lambda: set_copy(0, zz, r).wait_send(), lambda: set_copy(1, zz, r).wait_send())
    for p in range(NZ):
        zz = plane_at(p)
        for j in range(PLANE):
            for r in range(E_PARTS[p]):
                if j:
                    @pl.when(~is_end | (p < NZ - 1))
                    def _():
                        enc_copy(zz, j, r, E_PARTS[p]).wait_send()
                half_copy(zz * PLANE + j, r, E_PARTS[p], h).wait_send()

    @pl.when(~is_end)
    def _():
        for j in range(PLANE):
            for r in range(E_PARTS[-1]):
                if j:
                    pass_copy(j, r, E_PARTS[-1]).wait_send()
                last_copy(j, r, E_PARTS[-1]).wait_send()

    for c in range(groups):
        swap(c).wait_send()


def local_small(queries, key_weight, value_weight, out_weight, database, neighbours, placement):
    n = NZ * PLANE
    tok, width = queries.shape
    blk, half, de = database.shape
    feats = out_weight.shape[0] // 2
    groups = tok // CH
    hbm = pl.BlockSpec(memory_space=pl.ANY)
    dma = pltpu.SemaphoreType.DMA
    bf16 = jnp.bfloat16
    return pl.pallas_call(
        fused_kernel,
        out_shape=pltpu.VMEM((tok, feats), bf16),
        in_specs=[hbm] * 7,
        out_specs=pl.BlockSpec(memory_space=pltpu.VMEM),
        scratch_shapes=[
            pltpu.SMEM((KNB, neighbours.shape[0]), jnp.int32),
            pltpu.SMEM(placement.shape, jnp.int32),
            pltpu.VMEM((2, n) + key_weight.shape, bf16),
            pltpu.VMEM((NZ,) + database.shape, bf16),
            pltpu.VMEM((n, half, de), bf16),
            pltpu.VMEM((n, 2, half, de), bf16),
            pltpu.VMEM((PLANE, half, de), bf16),
            pltpu.VMEM((PLANE, half, de), bf16),
            pltpu.VMEM((2, n, 2, half, width), bf16),
            pltpu.VMEM((groups, CH, width), bf16),
            pltpu.VMEM((2, tok, width), bf16),
            pltpu.VMEM((feats, width), bf16),
            pltpu.VMEM((feats, width), bf16),
            dma((2, NZ, Z_PARTS)), dma((NZ, Z_PARTS)), dma((n, max(E_PARTS))), dma((n, max(E_PARTS))),
            dma((n, max(E_PARTS))), dma((n, max(E_PARTS))), dma((2, 2, NZ)), dma((2, 2, NZ)), dma((2, NZ)),
            dma((2, PLANE - 1)), dma((2, n)), dma((2,)),
            *[dma((PLANE, max(E_PARTS)))] * 3, dma((groups,)), dma((groups,)), dma((7,)),
            pltpu.SemaphoreType.REGULAR,
        ],
        compiler_params=pltpu.CompilerParams(
            collective_id=0, has_side_effects=True, vmem_limit_bytes=VMEM_LIMIT),
    )(neighbours.T, placement, queries.reshape(groups, CH, width), key_weight, value_weight, out_weight, database)


def local_general(queries, key_weight, value_weight, out_weight, database, neighbours, placement):
    shard_count = lax.axis_size("shard")
    shard_self = lax.axis_index("shard")
    tok_rows = queries.shape[0]
    hd_local = queries.shape[1]
    heads_local = hd_local // HD
    per_dev = tok_rows // CH
    blk_local = database.shape[0]
    slots = placement[neighbours]
    needed = slots.reshape(shard_count, per_dev * KNB)
    owners = needed // blk_local
    matches = owners == shard_self
    hits = jnp.any(matches, axis=1)
    which = jnp.sum(jnp.where(matches, needed % blk_local, 0), axis=1)
    outgoing = jnp.zeros((shard_count,) + database.shape[1:], jnp.bfloat16)
    for b in range(blk_local):
        taken = (hits & (which == b))[:, None, None]
        outgoing = jnp.where(taken, database[b][None], outgoing)
    arrived = lax.all_to_all(outgoing, "shard", split_axis=0, concat_axis=0, tiled=True)
    own_need = lax.dynamic_slice_in_dim(needed, shard_self, 1, 0)[0]
    half_rows = jnp.concatenate(
        [
            lax.dynamic_slice_in_dim(arrived, own_need[i] // blk_local, 1, 0)
            for i in range(per_dev * KNB)
        ],
        axis=0,
    )
    encoded = lax.all_gather(half_rows, "head", axis=1, tiled=True)
    key_rows, val_rows = (
        lax.all_gather(key_weight, "shard", axis=0, tiled=True),
        lax.all_gather(value_weight, "shard", axis=0, tiled=True),
    )
    key_block = jnp.einsum(
        "brd,de->bre", encoded, key_rows, preferred_element_type=jnp.float32
    ).astype(jnp.bfloat16)
    val_block = jnp.einsum(
        "brd,de->bre", encoded, val_rows, preferred_element_type=jnp.float32
    ).astype(jnp.bfloat16)
    neighbour_len = encoded.shape[1]
    key_heads = key_block.reshape(per_dev, KNB * neighbour_len, heads_local, HD)
    val_heads = val_block.reshape(per_dev, KNB * neighbour_len, heads_local, HD)
    query_pad = jnp.concatenate(
        [queries[CH - 1 :], jnp.zeros((CH - 1, hd_local), jnp.bfloat16)], axis=0
    )
    query_pad = query_pad.reshape(per_dev, CH, heads_local, HD)
    score_scale = HD ** (-0.5)
    scores = (
        jnp.einsum("swhd,skhd->shwk", query_pad, key_heads, preferred_element_type=jnp.float32)
        * score_scale
    )
    row_max = jnp.max(scores, axis=-1, keepdims=True)
    expo = jnp.exp(scores - row_max)
    probs = expo / jnp.sum(expo, axis=-1, keepdims=True)
    weights_bf = probs.astype(jnp.bfloat16)
    window_out = jnp.einsum(
        "shwk,skhd->swhd", weights_bf, val_heads, preferred_element_type=jnp.float32
    )
    window_rows = window_out.astype(jnp.bfloat16).reshape(tok_rows, hd_local)
    attention = jnp.concatenate(
        [jnp.zeros((CH - 1, hd_local), jnp.bfloat16), window_rows[: tok_rows - (CH - 1)]], axis=0
    )
    partial_value = lax.dot_general(
        attention, out_weight, (((1,), (1,)), ((), ())), preferred_element_type=jnp.float32
    )
    return lax.psum_scatter(partial_value, "head", scatter_dimension=1, tiled=True).astype(
        jnp.bfloat16
    )


def solution(mesh):
    sizes = dict(mesh.shape)
    small = sizes["shard"] == NZ * PLANE and sizes["head"] == 2
    return jax.shard_map(
        local_small if small else local_general,
        mesh=mesh,
        in_specs=(
            P("shard", "head"),
            P("shard", "head"),
            P("shard", "head"),
            P(None, "head"),
            P("shard", "head", None),
            P(),
            P(),
        ),
        out_specs=P("shard", "head"),
        check_vma=False,
    )
```
